32 devices in a mesh: wave: 8 (over z, x), lev: 4 (over y, core).
Axes of the slice: x: 2, y: 2, z: 4, core: 2. Of those that a mesh axis runs over, the one named last changes fastest.
Arguments:
- spectrum: bfloat16 [1024, 1024, 96, 6], P('wave', None, 'lev'), may hold values from -0.3125 to 0.3125
- legendre: bfloat16 [1024, 1024, 16], P('wave'), may hold values from -0.1875 to 0.1875
- wave_numbers: int32 [1024], replicated, may hold values from 0 to 1023, as said below
- vertical: float32 [96, 96], replicated, may hold values from -0.625 to 0.625
Outputs:
- tracer: float32 [96, 32, 2048], P(None, 'wave', 'lev')
The draws below stay inside these ranges and needn't reach their ends.
Inputs may be any that keep to these rules, and one draw needn't show every extreme that they name: wave_numbers is a permutation of 0 to 1023 in which slots 2 i and 2 i + 1 hold m and 1023 - m for some m, in either order.
All inputs are finite; a program needn't handle non-finite values.
Results may differ from the reference program's by a relative error of at most 0.0066.
Values may be sent and summed in bfloat16 or wider, within the bound.
No kernel may reach another device: no remote copies, remote signals or barrier semaphores. Data moves between devices by JAX's collectives and lax.ppermute only.
A program may use at most 256 MiB of HBM per device.

```python
import math
import jax
import jax.numpy as jnp
from jax import lax

NM = 1024
LEV = 96
NLAT = 32
NLON = 2048


def draw_wave_numbers(key, part):
    order = jax.random.permutation(jax.random.fold_in(key, 11), NM // 2).astype(jnp.int32)
    flipped = jax.random.randint(jax.random.fold_in(key, 23), (NM // 2,), 0, 2).astype(jnp.int32)
    partner = (NM - 1 - order).astype(jnp.int32)
    leading = jnp.where(flipped == 1, partner, order)
    trailing = jnp.where(flipped == 1, order, partner)
    return jnp.stack([leading, trailing], axis=1).reshape(NM).astype(jnp.int32)


def block_levels(rng, extent, pieces, low, top_value):
    gain, own = 1.0, jax.random.fold_in(rng, 6)
    for position, shards_of in pieces:
        draws = jnp.exp(jax.random.uniform(jax.random.fold_in(own, position), (shards_of,), jnp.float32, low / len(pieces), top_value / len(pieces)))
        gain = gain * jnp.repeat(draws, extent[position] // shards_of).reshape([-1 if axis == position else 1 for axis in range(len(extent))])
    return gain


def gaussian(key, dims, deviation, bound, cuts=(), kind=jnp.bfloat16):
    values = jax.random.normal(key, dims, jnp.float32) * deviation
    if len(cuts) > 0:
        values = block_levels(key, dims, cuts, -0.22, 0.18) * values
    return jnp.clip(values, min=-bound, max=bound).astype(kind)


def setup_inputs(seed: int = 0) -> dict:
    seeds = jax.random.split(jax.random.key(seed), 5)
    return {
        "spectrum": gaussian(seeds[0], (NM, NM, LEV, 6), (0.7 / NM ** 0.5), 0.3125, ((0, 8), (2, 4))),
        "legendre": gaussian(seeds[1], (NM, NM, NLAT // 2), NM ** -0.5, 0.1875, ((0, 8),)),
        "wave_numbers": draw_wave_numbers(jax.random.fold_in(seeds[4], 71), 0),
        "vertical": gaussian(seeds[3], (LEV, LEV), LEV ** -0.5, 0.625, (), jnp.float32),
    }


courant_max = 0.45


def triangle_sums(spectrum_block, legendre_block, numbers):
    degree_count = spectrum_block.shape[1]
    degree = jnp.arange(degree_count, dtype=jnp.int32)
    counted = degree[None, :] < (degree_count - numbers)[:, None]
    even_mask = counted & (degree[None, :] % 2 == 0)
    odd_mask = counted & (degree[None, :] % 2 == 1)
    coefficient = spectrum_block.reshape(spectrum_block.shape[0], degree_count, -1).astype(jnp.float32)
    basis = legendre_block.astype(jnp.float32)
    zero_value = jnp.zeros((), jnp.float32)
    even_sums = jnp.einsum('skc,ski->sci', jnp.where(even_mask[:, :, None], coefficient, zero_value), basis)
    odd_sums = jnp.einsum('skc,ski->sci', jnp.where(odd_mask[:, :, None], coefficient, zero_value), basis)
    northern = even_sums + odd_sums
    southern = jnp.flip(even_sums - odd_sums, axis=2)
    return jnp.concatenate([northern, southern], axis=2).astype(jnp.bfloat16)


def twiddles(numbers):
    longitude = jnp.arange(NLON, dtype=jnp.int32)
    residue = (numbers[:, None] * longitude[None, :]) % NLON
    angles = residue.astype(jnp.float32) * (2.0 * math.pi / NLON)
    weight = jnp.where(numbers == 0, 1.0, 2.0).astype(jnp.float32)[:, None]
    return jnp.stack([weight * jnp.cos(angles), -weight * jnp.sin(angles)]).astype(jnp.bfloat16)


def upwind_core(extended, courant_x, courant_y):
    center = extended[:, 1:-1, 1:-1]
    western = extended[:, 1:-1, :-2]
    eastern = extended[:, 1:-1, 2:]
    northern = extended[:, :-2, 1:-1]
    southern = extended[:, 2:, 1:-1]
    return (center - jnp.maximum(courant_x, 0.0) * (center - western)
            - jnp.minimum(courant_x, 0.0) * (eastern - center)
            - jnp.maximum(courant_y, 0.0) * (center - northern)
            - jnp.minimum(courant_y, 0.0) * (southern - center))


def extend(field):
    padded = jnp.pad(field, ((0, 0), (1, 1), (0, 0)))
    return jnp.concatenate([padded[:, :, -1:], padded, padded[:, :, :1]], axis=2)


def reference(spectrum, legendre, wave_numbers, vertical):
    group = 16
    spectrum_blocks = spectrum.reshape(NM // group, group, NM, LEV * 6)
    legendre_blocks = legendre.reshape(NM // group, group, NM, NLAT // 2)
    number_blocks = wave_numbers.reshape(NM // group, group)
    fourier = lax.map(lambda packed: triangle_sums(packed[0], packed[1], packed[2]),
                      (spectrum_blocks, legendre_blocks, number_blocks))
    mode_groups = LEV // 16
    fourier = fourier.reshape(NM, mode_groups, 16, 3, 2, NLAT)
    fourier = jnp.moveaxis(fourier, 1, 0)
    twiddle = twiddles(wave_numbers).astype(jnp.float32)
    vertical_groups = jnp.moveaxis(vertical.reshape(LEV, mode_groups, 16), 1, 0)

    def accumulate(carry, packed):
        block, vertical_part = packed
        grid_values = jnp.einsum('smfrl,rsj->lmfj', block.astype(jnp.float32), twiddle)
        grid_values = grid_values.astype(jnp.bfloat16)
        term = jnp.einsum('vm,lmfj->fvlj', vertical_part, grid_values.astype(jnp.float32),
                          precision=lax.Precision.HIGHEST)
        return carry + term, None

    fields, _ = lax.scan(accumulate, jnp.zeros((3, LEV, NLAT, NLON), jnp.float32),
                         (fourier, vertical_groups))
    courant_x = courant_max * jnp.tanh(fields[0])
    courant_y = courant_max * jnp.tanh(fields[1])
    tracer = fields[2]
    for sweep in range(2):
        tracer = upwind_core(extend(tracer), courant_x, courant_y)
    return tracer
```

```python
import functools
import math

import jax
import jax.numpy as jnp
from jax import lax
from jax.experimental import pallas as pl
from jax.experimental.pallas import tpu as pltpu
from jax.sharding import PartitionSpec as P

NLON = 2048
FIELDS = 3
PARTS = 2
LANES = 128
CHUNK = 256
TILE = 256

courant_max = 0.45


def padded(block, sides, width, periodic):
    for axis, dim in sides:
        count = lax.axis_size(axis)
        forward = [(i, i + 1) for i in range(count - 1)]
        if periodic:
            forward.append((count - 1, 0))
        backward = [(target, source) for source, target in forward]
        low = lax.ppermute(
            lax.slice_in_dim(block, block.shape[dim] - width, None, axis=dim), axis, forward
        )
        high = lax.ppermute(lax.slice_in_dim(block, 0, width, axis=dim), axis, backward)
        block = jnp.concatenate([low, block, high], axis=dim)
    return block


def twiddles(numbers):
    longitude = jnp.arange(NLON, dtype=jnp.int32)
    residue = numbers[:, None] * longitude[None, :] % NLON
    angles = residue.astype(jnp.float32) * (2.0 * math.pi / NLON)
    weight = jnp.where(numbers == 0, 1.0, 2.0).astype(jnp.float32)[:, None]
    return jnp.stack([weight * jnp.cos(angles), -weight * jnp.sin(angles)]).astype(jnp.bfloat16)


def parity_columns(coefficient, degree, lengths):
    counted = degree < lengths[:, None]
    even_mask = counted & (degree % 2 == 0)
    odd_mask = counted & (degree % 2 == 1)
    return jnp.concatenate(
        [
            jnp.where(even_mask[:, :, None], coefficient, 0),
            jnp.where(odd_mask[:, :, None], coefficient, 0),
        ],
        axis=2,
    )


def padded_sums(coefficient, basis, own_numbers):
    degree_count = coefficient.shape[1]
    degree = jnp.arange(degree_count, dtype=jnp.int32)[None, :]
    masked = parity_columns(coefficient, degree, degree_count - own_numbers)
    return jnp.einsum("skc,ski->sci", masked, basis, preferred_element_type=jnp.float32)


def upwind_core(extended, courant_x, courant_y):
    center = extended[:, 1:-1, 1:-1]
    western = extended[:, 1:-1, :-2]
    eastern = extended[:, 1:-1, 2:]
    northern = extended[:, :-2, 1:-1]
    southern = extended[:, 2:, 1:-1]
    return (
        center
        - jnp.maximum(courant_x, 0.0) * (center - western)
        - jnp.minimum(courant_x, 0.0) * (eastern - center)
        - jnp.maximum(courant_y, 0.0) * (center - northern)
        - jnp.minimum(courant_y, 0.0) * (southern - center)
    )


def plain_body(spectrum, legendre, wave_numbers, vertical):
    slot_count, degree_count, level_count, part_count = spectrum.shape
    columns = level_count * part_count
    coefficient = spectrum.reshape(slot_count, degree_count, columns)
    first_slot = lax.axis_index("wave") * slot_count
    own_numbers = lax.dynamic_slice_in_dim(wave_numbers, first_slot, slot_count)
    partial_sums = padded_sums(coefficient, legendre, own_numbers)
    even_sums = partial_sums[:, :columns]
    odd_sums = partial_sums[:, columns:]
    northern = even_sums + odd_sums
    southern = jnp.flip(even_sums - odd_sums, axis=2)
    fourier = jnp.concatenate([northern, southern], axis=2).astype(jnp.bfloat16)
    received = lax.all_to_all(fourier, "wave", split_axis=2, concat_axis=0, tiled=True)
    lat_count = received.shape[2]
    received = received.reshape(received.shape[0], level_count, FIELDS, PARTS, lat_count)
    twiddle = twiddles(wave_numbers)
    grid_values = jnp.einsum(
        "smfrl,rsj->lmfj", received, twiddle, preferred_element_type=jnp.float32
    ).astype(jnp.bfloat16)
    column_values = lax.all_to_all(grid_values, "lev", split_axis=3, concat_axis=1, tiled=True)
    fields = jnp.einsum(
        "vm,lmfj->fvlj",
        vertical,
        column_values.astype(jnp.float32),
        precision=lax.Precision.HIGHEST,
    )
    courant_x = courant_max * jnp.tanh(fields[0])
    courant_y = courant_max * jnp.tanh(fields[1])
    tracer = fields[2]
    for sweep in range(2):
        extended = padded(tracer, (("wave", 1),), 1, False)
        extended = padded(extended, (("lev", 2),), 1, True)
        tracer = upwind_core(extended, courant_x, courant_y)
    return tracer


def vmem():
    return pl.BlockSpec(memory_space=pltpu.VMEM)


def cost(flops, count_bytes):
    return pl.CostEstimate(flops=flops, bytes_accessed=count_bytes, transcendentals=0)


def legendre_kernel(
    waves, lats, modes, pairs, numbers_ref, place_ref, spectrum_ref, legendre_ref, *refs
):
    outs, (held, sums, arrived) = refs[:-3], refs[-3:]
    half = legendre_ref.shape[1]
    degrees = legendre_ref.shape[2]
    rows = spectrum_ref.shape[1]
    slots = spectrum_ref.shape[0]
    chunks = degrees // CHUNK + 1
    step, steps = pl.program_id(0), pl.num_programs(0)

    def plan(pair):
        first = degrees - numbers_ref[2 * pair]
        second = degrees - numbers_ref[2 * pair + 1]
        return first, second, (first + CHUNK - 1) // CHUNK

    def copy(group, slot, pair, t):
        index = group * pairs + pair
        _, _, edge = plan(index)
        inside = t < edge
        source = 2 * index + jnp.where(inside, 0, 1)
        block = jnp.where(inside, t, t - edge)
        start = pl.multiple_of(block * CHUNK, CHUNK)
        return pltpu.make_async_copy(
            spectrum_ref.at[source, :, pl.ds(start, CHUNK)],
            held.at[slot, pair, :, pl.ds(t * CHUNK, CHUNK)],
            arrived.at[slot],
        )

    def fetch(group, slot):
        for pair in range(pairs):
            for t in range(chunks):
                copy(group, slot, pair, t).start()

    @pl.when(step == 0)
    def _():
        fetch(0, 0)

    now = lax.rem(step, 2)

    @pl.when(step + 1 < steps)
    def _():
        fetch(step + 1, 1 - now)

    for pair in range(pairs):
        for t in range(chunks):
            copy(step, now, pair, t).wait()

    lane = lax.broadcasted_iota(jnp.int32, (half, CHUNK), 1)
    sign = jnp.where(lane % 2 == 0, 1.0, -1.0)
    for pair in range(pairs):
        index = step * pairs + pair
        first, second, edge = plan(index)
        columns = []
        for t in range(chunks):
            inside = t < edge
            local = 2 * pair + jnp.where(inside, 0, 1)
            block = jnp.where(inside, t, t - edge)
            start = pl.multiple_of(block * CHUNK, CHUNK)
            length = jnp.where(inside, first, second) - start
            values = legendre_ref[local, :, pl.ds(start, CHUNK)].astype(jnp.float32)
            values = jnp.where(lane < length, values, 0.0)
            own = jnp.where(inside, 1.0, 0.0)
            north_first = values * own
            north_second = values - north_first
            columns.append(
                jnp.concatenate(
                    [
                        north_first,
                        north_first * sign,
                        north_second,
                        north_second * sign,
                    ],
                    axis=0,
                ).astype(jnp.bfloat16)
            )
        basis = jnp.concatenate(columns, axis=1)
        result = lax.dot_general(
            basis,
            held[now, pair],
            (((1,), (1,)), ((), ())),
            preferred_element_type=jnp.float32,
        )
        for which in range(2):
            part = result[which * 2 * half : (which + 1) * 2 * half]
            for low in range(0, rows, LANES):
                width = min(LANES, rows - low)
                sums[low // LANES, pl.ds(2 * index + which, 2 * half, stride=slots), :width] = part[
                    :, low : low + width
                ]

    @pl.when(step == steps - 1)
    def _():
        place = place_ref[0]
        for d in range(waves):
            for l in range(lats):
                lat = (place ^ d) * lats + l
                row = jnp.where(lat < half, lat, 3 * half - 1 - lat)
                start = pl.multiple_of(row * slots, slots)
                turned = [
                    sums[low // LANES, pl.ds(start, slots), :].T.astype(jnp.bfloat16)
                    for low in range(0, rows, LANES)
                ]
                whole = jnp.concatenate(turned, axis=0)
                for f in range(FIELDS):
                    for p in range(PARTS):
                        base = (f * PARTS + p) * modes
                        outs[f * waves + d][p, l] = whole[base : base + modes]


def legendre_stage(spectrum, legendre, own_numbers, place, waves):
    slots, degrees, modes, _ = spectrum.shape
    half = legendre.shape[2]
    lats = 2 * half // waves
    rows = modes * FIELDS * PARTS
    turned = jnp.transpose(spectrum, (0, 3, 2, 1)).reshape(slots, rows, degrees)
    basis = jnp.transpose(legendre, (0, 2, 1))
    pairs = 4
    chunks = degrees // CHUNK + 1
    outs = [jax.ShapeDtypeStruct((PARTS, lats, modes, slots), jnp.bfloat16)] * (FIELDS * waves)
    tiles = -(-rows // LANES)
    return pl.pallas_call(
        functools.partial(legendre_kernel, waves, lats, modes, pairs),
        out_shape=outs,
        grid_spec=pltpu.PrefetchScalarGridSpec(
            num_scalar_prefetch=2,
            grid=(slots // (2 * pairs),),
            in_specs=[
                pl.BlockSpec(memory_space=pl.ANY),
                pl.BlockSpec((2 * pairs, half, degrees), lambda i, *_: (i, 0, 0)),
            ],
            out_specs=[
                pl.BlockSpec((PARTS, lats, modes, slots), lambda i, *_: (0, 0, 0, 0))
                for _ in outs
            ],
            scratch_shapes=[
                pltpu.VMEM((2, pairs, rows, chunks * CHUNK), jnp.bfloat16),
                pltpu.VMEM((tiles, 2 * half * slots, LANES), jnp.float32),
                pltpu.SemaphoreType.DMA((2,)),
            ],
        ),
        compiler_params=pltpu.CompilerParams(dimension_semantics=("arbitrary",)),
        cost_estimate=cost(slots * rows * degrees * 2 * half, slots * rows * degrees),
        name="legendre_sums",
    )(own_numbers, place, turned, basis)


def twiddle_kernel(low_cos_ref, low_sin_ref, high_cos_ref, high_sin_ref, out_ref):
    low_cos, low_sin = low_cos_ref[0], low_sin_ref[0]
    for block in range(out_ref.shape[3] // LANES):
        high_cos = high_cos_ref[0, :, block : block + 1]
        high_sin = high_sin_ref[0, :, block : block + 1]
        lanes = pl.ds(block * LANES, LANES)
        out_ref[0, 0, :, lanes] = (high_cos * low_cos - high_sin * low_sin).astype(jnp.bfloat16)
        out_ref[0, 1, :, lanes] = -(high_sin * low_cos + high_cos * low_sin).astype(jnp.bfloat16)


def twiddle_stage(numbers):
    waves, slots = numbers.shape
    count = NLON // 2
    blocks = count // LANES

    def angles(steps):
        residue = numbers[:, :, None] * steps[None, None, :] % NLON
        return residue.astype(jnp.float32) * (2.0 * math.pi / NLON)

    low = angles(jnp.arange(LANES, dtype=jnp.int32))
    high = angles(jnp.arange(blocks, dtype=jnp.int32) * LANES)
    weight = jnp.where(numbers == 0, 1.0, 2.0).astype(jnp.float32)[:, :, None]

    def spec(last):
        return pl.BlockSpec((1, slots, last), lambda i: (i, 0, 0))

    return pl.pallas_call(
        twiddle_kernel,
        out_shape=jax.ShapeDtypeStruct((waves, PARTS, slots, count), jnp.bfloat16),
        grid=(waves,),
        in_specs=[spec(LANES), spec(LANES), spec(blocks), spec(blocks)],
        out_specs=pl.BlockSpec((1, PARTS, slots, count), lambda i: (i, 0, 0, 0)),
        cost_estimate=cost(8 * waves * slots * count, 4 * waves * slots * count),
        name="twiddles",
    )(jnp.cos(low), jnp.sin(low), weight * jnp.cos(high), weight * jnp.sin(high))


def synthesis_kernel(waves, levs, place_ref, *refs):
    blocks, (sign_ref, twiddle_ref) = refs[:waves], refs[waves : waves + 2]
    outs, (left, grid) = refs[waves + 2 : -2], refs[-2:]
    _, lats, modes, slots = blocks[0].shape
    rows = lats * modes
    step, steps = pl.program_id(0), pl.num_programs(0)

    @pl.when(step == 0)
    def _():
        for d in range(waves):
            sign = sign_ref[d]
            for p in range(PARTS):
                values = blocks[d][p].reshape(rows, slots)
                lanes = pl.ds((d * PARTS + p) * slots, slots)
                left[:rows, lanes] = values
                left[rows:, lanes] = values * sign

    right = twiddle_ref[...].reshape(waves * PARTS * slots, TILE)
    result = jnp.dot(left[...], right, preferred_element_type=jnp.float32).astype(jnp.bfloat16)
    width = NLON // levs
    ratio = width // TILE
    lane = lax.broadcasted_iota(jnp.int32, (rows, LANES), 1)
    for which in range(2):
        values = result[which * rows : (which + 1) * rows]
        block = step + which * steps
        owner = block // ratio
        inner = lax.rem(block, ratio)
        start = pl.multiple_of(inner * TILE, TILE)
        grid[owner, :, pl.ds(start, TILE)] = values

        @pl.when(inner == 0)
        def _():
            west = lax.rem(owner + levs - 1, levs)
            grid[west, :, pl.ds(width, LANES)] = jnp.where(
                lane < LANES // 2, values[:, :LANES], grid[west, :, pl.ds(width, LANES)]
            )

        @pl.when(inner == ratio - 1)
        def _():
            east = lax.rem(owner + 1, levs)
            grid[east, :, pl.ds(width, LANES)] = jnp.where(
                lane < LANES // 2, grid[east, :, pl.ds(width, LANES)], values[:, -LANES:]
            )

    @pl.when(step == steps - 1)
    def _():
        place = place_ref[0]
        for e in range(levs):
            outs[e][...] = grid[place ^ e]


def synthesis_stage(blocks, sign, twiddle, place, levs):
    waves, _, slots, count = twiddle.shape
    _, lats, modes, _ = blocks[0].shape
    rows = lats * modes
    width = NLON // levs + LANES
    depth = waves * PARTS * slots
    return pl.pallas_call(
        functools.partial(synthesis_kernel, waves, levs),
        out_shape=[jax.ShapeDtypeStruct((rows, width), jnp.bfloat16)] * levs,
        grid_spec=pltpu.PrefetchScalarGridSpec(
            num_scalar_prefetch=1,
            grid=(count // TILE,),
            in_specs=[
                pl.BlockSpec((PARTS, lats, modes, slots), lambda i, *_: (0, 0, 0, 0))
                for _ in blocks
            ]
            + [
                pl.BlockSpec((waves, 1, slots), lambda i, *_: (0, 0, 0)),
                pl.BlockSpec((waves, PARTS, slots, TILE), lambda i, *_: (0, 0, 0, i)),
            ],
            out_specs=[pl.BlockSpec((rows, width), lambda i, *_: (0, 0))] * levs,
            scratch_shapes=[
                pltpu.VMEM((2 * rows, depth), jnp.bfloat16),
                pltpu.VMEM((levs, rows, width), jnp.bfloat16),
            ],
        ),
        compiler_params=pltpu.CompilerParams(dimension_semantics=("arbitrary",)),
        cost_estimate=cost(4 * rows * depth * count, 2 * depth * count),
        name="synthesis",
    )(place, *blocks, sign, twiddle)


def three_terms(matrix):
    high = matrix.astype(jnp.bfloat16)
    rest = matrix - high.astype(jnp.float32)
    middle = rest.astype(jnp.bfloat16)
    low = (rest - middle.astype(jnp.float32)).astype(jnp.bfloat16)
    return jnp.concatenate([high, middle, low], axis=0)


def levels_of(terms, blocks, lat, modes):
    count = terms.shape[0] // 3
    rows = jnp.concatenate(
        [block[lat * modes : (lat + 1) * modes].astype(jnp.float32) for block in blocks], axis=0
    ).astype(jnp.bfloat16)
    result = jnp.dot(terms, rows, preferred_element_type=jnp.float32)
    return result[:count] + (result[count : 2 * count] + result[2 * count :])


def tracer_kernel(modes, vertical_ref, *refs):
    blocks, (field_ref, north_ref, south_ref) = refs[:-3], refs[-3:]
    terms = three_terms(vertical_ref[...])
    lats = field_ref.shape[0]
    for lat in range(lats):
        values = levels_of(terms, blocks, lat, modes)
        field_ref[lat] = values
        if lat == 0:
            north_ref[...] = values.astype(jnp.bfloat16)
        if lat == lats - 1:
            south_ref[...] = values.astype(jnp.bfloat16)


def courant_kernel(modes, vertical_ref, *refs):
    blocks, field_ref = refs[:-1], refs[-1]
    terms = three_terms(vertical_ref[...])
    for lat in range(field_ref.shape[0]):
        field_ref[lat] = courant_max * jnp.tanh(levels_of(terms, blocks, lat, modes))


def upwind(center, western, eastern, northern, southern, courant_x, courant_y):
    return (
        center
        - jnp.maximum(courant_x, 0.0) * (center - western)
        - jnp.minimum(courant_x, 0.0) * (eastern - center)
        - jnp.maximum(courant_y, 0.0) * (center - northern)
        - jnp.minimum(courant_y, 0.0) * (southern - center)
    )


def stepped(lat, tracer_ref, above_ref, below_ref, courant_x, courant_y):
    lats, _, width = tracer_ref.shape
    center = tracer_ref[lat]
    northern = tracer_ref[lat - 1] if lat > 0 else above_ref[...].astype(jnp.float32)
    southern = tracer_ref[lat + 1] if lat < lats - 1 else below_ref[...].astype(jnp.float32)
    return upwind(
        center,
        pltpu.roll(center, 1, 1),
        pltpu.roll(center, width - 1, 1),
        northern,
        southern,
        courant_x,
        courant_y,
    )


def first_step_kernel(modes, vertical_ref, tracer_ref, above_ref, below_ref, x_ref, *refs):
    blocks, (y_ref, out_ref, north_ref, south_ref) = refs[:-4], refs[-4:]
    terms = three_terms(vertical_ref[...])
    lats = tracer_ref.shape[0]
    for lat in range(lats):
        courant_y = courant_max * jnp.tanh(levels_of(terms, blocks, lat, modes))
        y_ref[lat] = courant_y
        values = stepped(lat, tracer_ref, above_ref, below_ref, x_ref[lat], courant_y)
        out_ref[lat] = values
        if lat == 0:
            north_ref[...] = values.astype(jnp.bfloat16)
        if lat == lats - 1:
            south_ref[...] = values.astype(jnp.bfloat16)


def second_step_kernel(tracer_ref, above_ref, below_ref, x_ref, y_ref, out_ref):
    width = out_ref.shape[2]
    for lat in range(tracer_ref.shape[0]):
        values = stepped(lat, tracer_ref, above_ref, below_ref, x_ref[lat], y_ref[lat])
        out_ref[:, lat, :] = values[:, :width]


def local_call(kernel, outs, name, *operands):
    return pl.pallas_call(
        kernel,
        out_shape=outs,
        in_specs=[vmem() for _ in operands],
        out_specs=jax.tree.map(lambda _: vmem(), outs),
        cost_estimate=cost(4_000_000, 4_000_000),
        name=name,
    )(*operands)


def exchange(blocks, axis):
    count = lax.axis_size(axis)
    return [blocks[0]] + [
        lax.ppermute(blocks[d], axis, [(i, i ^ d) for i in range(count)]) for d in range(1, count)
    ]


def edges(north, south):
    count = lax.axis_size("wave")
    above = lax.ppermute(south, "wave", [(i, i + 1) for i in range(count - 1)])
    below = lax.ppermute(north, "wave", [(i + 1, i) for i in range(count - 1)])
    return above, below


def tiled_body(spectrum, legendre, wave_numbers, vertical):
    waves, levs = lax.axis_size("wave"), lax.axis_size("lev")
    slots, degrees, modes, _ = spectrum.shape
    levels = vertical.shape[0]
    lats = 2 * legendre.shape[2] // waves
    width = NLON // levs
    wave_place, lev_place = lax.axis_index("wave"), lax.axis_index("lev")
    by_wave = wave_numbers.reshape(waves, slots)[wave_place ^ jnp.arange(waves)]
    by_lev = vertical.reshape(levels, levs, modes)[:, lev_place ^ jnp.arange(levs)]
    by_lev = by_lev.reshape(levels, levs * modes)
    sign = jnp.where(by_wave % 2 == 0, 1.0, -1.0).astype(jnp.bfloat16)[:, None, :]

    fourier = legendre_stage(spectrum, legendre, by_wave[0], wave_place[None], waves)
    twiddle = twiddle_stage(by_wave)
    columns = {}
    for field in (2, 0, 1):
        received = exchange(fourier[field * waves : (field + 1) * waves], "wave")
        grid = synthesis_stage(received, sign, twiddle, lev_place[None], levs)
        columns[field] = exchange(grid, "lev")

    whole = jax.ShapeDtypeStruct((lats, levels, width + LANES), jnp.float32)
    row = jax.ShapeDtypeStruct((levels, width + LANES), jnp.bfloat16)
    tracer, north, south = local_call(
        functools.partial(tracer_kernel, modes), (whole, row, row), "tracer", by_lev, *columns[2]
    )
    above, below = edges(north, south)
    courant_x = local_call(
        functools.partial(courant_kernel, modes), whole, "courant_x", by_lev, *columns[0]
    )
    courant_y, tracer, north, south = local_call(
        functools.partial(first_step_kernel, modes),
        (whole, whole, row, row),
        "first_step",
        by_lev,
        tracer,
        above,
        below,
        courant_x,
        *columns[1],
    )
    above, below = edges(north, south)
    return local_call(
        second_step_kernel,
        jax.ShapeDtypeStruct((levels, lats, width), jnp.float32),
        "second_step",
        tracer,
        above,
        below,
        courant_x,
        courant_y,
    )


def body(spectrum, legendre, wave_numbers, vertical):
    waves, levs = lax.axis_size("wave"), lax.axis_size("lev")
    slots, degrees, modes, _ = spectrum.shape
    tiled = (
        slots % LANES == 0
        and modes % 8 == 0
        and degrees % CHUNK == 0
        and waves & (waves - 1) == 0
        and levs & (levs - 1) == 0
        and NLON // levs % TILE == 0
        and levs % 2 == 0
    )
    form = tiled_body if tiled else plain_body
    return form(spectrum, legendre, wave_numbers, vertical)


def solution(mesh):
    in_specs = (P("wave", None, "lev", None), P("wave", None, None), P(), P())
    out_specs = P(None, "wave", "lev")
    return jax.shard_map(body, mesh=mesh, in_specs=in_specs, out_specs=out_specs, check_vma=False)
```

```python
import functools
import math

import jax
import jax.numpy as jnp
from jax import lax
from jax.experimental import pallas as pl
from jax.experimental.pallas import tpu as pltpu
from jax.sharding import PartitionSpec as P

NLON = 2048
FIELDS = 3
PARTS = 2
LANES = 128
CHUNK = 256
TILE = 256
PAIRS = 4

courant_max = 0.45


def padded(block, sides, width, periodic):
    for axis, dim in sides:
        count = lax.axis_size(axis)
        forward = [(i, i + 1) for i in range(count - 1)]
        if periodic:
            forward.append((count - 1, 0))
        backward = [(target, source) for source, target in forward]
        low = lax.ppermute(
            lax.slice_in_dim(block, block.shape[dim] - width, None, axis=dim), axis, forward
        )
        high = lax.ppermute(lax.slice_in_dim(block, 0, width, axis=dim), axis, backward)
        block = jnp.concatenate([low, block, high], axis=dim)
    return block


def twiddles(numbers):
    longitude = jnp.arange(NLON, dtype=jnp.int32)
    residue = numbers[:, None] * longitude[None, :] % NLON
    angles = residue.astype(jnp.float32) * (2.0 * math.pi / NLON)
    weight = jnp.where(numbers == 0, 1.0, 2.0).astype(jnp.float32)[:, None]
    return jnp.stack([weight * jnp.cos(angles), -weight * jnp.sin(angles)]).astype(jnp.bfloat16)


def parity_columns(coefficient, degree, lengths):
    counted = degree < lengths[:, None]
    even_mask = counted & (degree % 2 == 0)
    odd_mask = counted & (degree % 2 == 1)
    return jnp.concatenate(
        [
            jnp.where(even_mask[:, :, None], coefficient, 0),
            jnp.where(odd_mask[:, :, None], coefficient, 0),
        ],
        axis=2,
    )


def padded_sums(coefficient, basis, own_numbers):
    degree_count = coefficient.shape[1]
    degree = jnp.arange(degree_count, dtype=jnp.int32)[None, :]
    masked = parity_columns(coefficient, degree, degree_count - own_numbers)
    return jnp.einsum("skc,ski->sci", masked, basis, preferred_element_type=jnp.float32)


def upwind_core(extended, courant_x, courant_y):
    center = extended[:, 1:-1, 1:-1]
    western = extended[:, 1:-1, :-2]
    eastern = extended[:, 1:-1, 2:]
    northern = extended[:, :-2, 1:-1]
    southern = extended[:, 2:, 1:-1]
    return (
        center
        - jnp.maximum(courant_x, 0.0) * (center - western)
        - jnp.minimum(courant_x, 0.0) * (eastern - center)
        - jnp.maximum(courant_y, 0.0) * (center - northern)
        - jnp.minimum(courant_y, 0.0) * (southern - center)
    )


def plain_body(spectrum, legendre, wave_numbers, vertical):
    slot_count, degree_count, level_count, part_count = spectrum.shape
    columns = level_count * part_count
    coefficient = spectrum.reshape(slot_count, degree_count, columns)
    first_slot = lax.axis_index("wave") * slot_count
    own_numbers = lax.dynamic_slice_in_dim(wave_numbers, first_slot, slot_count)
    partial_sums = padded_sums(coefficient, legendre, own_numbers)
    even_sums = partial_sums[:, :columns]
    odd_sums = partial_sums[:, columns:]
    northern = even_sums + odd_sums
    southern = jnp.flip(even_sums - odd_sums, axis=2)
    fourier = jnp.concatenate([northern, southern], axis=2).astype(jnp.bfloat16)
    received = lax.all_to_all(fourier, "wave", split_axis=2, concat_axis=0, tiled=True)
    lat_count = received.shape[2]
    received = received.reshape(received.shape[0], level_count, FIELDS, PARTS, lat_count)
    twiddle = twiddles(wave_numbers)
    grid_values = jnp.einsum(
        "smfrl,rsj->lmfj", received, twiddle, preferred_element_type=jnp.float32
    ).astype(jnp.bfloat16)
    column_values = lax.all_to_all(grid_values, "lev", split_axis=3, concat_axis=1, tiled=True)
    fields = jnp.einsum(
        "vm,lmfj->fvlj",
        vertical,
        column_values.astype(jnp.float32),
        precision=lax.Precision.HIGHEST,
    )
    courant_x = courant_max * jnp.tanh(fields[0])
    courant_y = courant_max * jnp.tanh(fields[1])
    tracer = fields[2]
    for sweep in range(2):
        extended = padded(tracer, (("wave", 1),), 1, False)
        extended = padded(extended, (("lev", 2),), 1, True)
        tracer = upwind_core(extended, courant_x, courant_y)
    return tracer


def vmem():
    return pl.BlockSpec(memory_space=pltpu.VMEM)


def cost(flops, count_bytes):
    return pl.CostEstimate(flops=flops, bytes_accessed=count_bytes, transcendentals=0)


def legendre_kernel(
    waves, lats, modes, pairs, numbers_ref, place_ref, spectrum_ref, legendre_ref, *refs
):
    outs, (held, sums, arrived) = refs[:-3], refs[-3:]
    half = legendre_ref.shape[1]
    degrees = legendre_ref.shape[2]
    slots, rows, _ = spectrum_ref.shape
    chunks = degrees // CHUNK + 1
    step, steps = pl.program_id(0), pl.num_programs(0)
    place = place_ref[0]

    def plan(index):
        first = degrees - numbers_ref[place * slots + 2 * index]
        second = degrees - numbers_ref[place * slots + 2 * index + 1]
        return first, second, lax.shift_right_logical(first + (CHUNK - 1), CHUNK.bit_length() - 1)

    def fetch(group, slot):
        for pair in range(pairs):
            index = group * pairs + pair
            _, _, edge = plan(index)
            for t in range(chunks):
                inside = t < edge
                source = jnp.where(inside, 2 * index, 2 * index + 1)
                block = jnp.where(inside, t, t - edge)
                start = pl.multiple_of(block * CHUNK, CHUNK)
                pltpu.make_async_copy(
                    spectrum_ref.at[source, :, pl.ds(start, CHUNK)],
                    held.at[slot, pair, :, pl.ds(t * CHUNK, CHUNK)],
                    arrived.at[slot],
                ).start()

    @pl.when(step == 0)
    def _():
        fetch(0, 0)

    now = lax.rem(step, 2)

    @pl.when(step + 1 < steps)
    def _():
        fetch(step + 1, 1 - now)

    pltpu.make_async_copy(held.at[now], held.at[now], arrived.at[now]).wait()

    lane = lax.broadcasted_iota(jnp.int32, (half, CHUNK), 1)
    sign = jnp.where(lane % 2 == 0, 1.0, -1.0)
    for pair in range(pairs):
        index = step * pairs + pair
        first, second, edge = plan(index)
        columns = []
        for t in range(chunks):
            inside = t < edge
            local = jnp.where(inside, 2 * pair, 2 * pair + 1)
            block = jnp.where(inside, t, t - edge)
            start = pl.multiple_of(block * CHUNK, CHUNK)
            length = jnp.where(inside, first, second) - start
            values = legendre_ref[local, :, pl.ds(start, CHUNK)].astype(jnp.float32)
            values = jnp.where(lane < length, values, 0.0)
            north_first = values * jnp.where(inside, 1.0, 0.0)
            north_second = values - north_first
            columns.append(
                jnp.concatenate(
                    [
                        north_first,
                        north_first * sign,
                        north_second,
                        north_second * sign,
                    ],
                    axis=0,
                ).astype(jnp.bfloat16)
            )
        basis = jnp.concatenate(columns, axis=1)
        result = lax.dot_general(
            basis,
            held[now, pair],
            (((1,), (1,)), ((), ())),
            preferred_element_type=jnp.float32,
        )
        for which in range(2):
            part = result[which * 2 * half : (which + 1) * 2 * half]
            for low in range(0, rows, LANES):
                width = min(LANES, rows - low)
                sums[low // LANES, pl.ds(2 * index + which, 2 * half, stride=slots), :width] = part[
                    :, low : low + width
                ]

    @pl.when(step == steps - 1)
    def _():
        for d in range(waves):
            for l in range(lats):
                lat = (place ^ d) * lats + l
                row = jnp.where(lat < half, lat, 3 * half - 1 - lat)
                start = pl.multiple_of(row * slots, slots)
                turned = [
                    sums[low // LANES, pl.ds(start, slots), :].T.astype(jnp.bfloat16)
                    for low in range(0, rows, LANES)
                ]
                whole = jnp.concatenate(turned, axis=0)
                for f in range(FIELDS):
                    for p in range(PARTS):
                        base = (f * PARTS + p) * modes
                        outs[d][f, p, l] = whole[base : base + modes]


def legendre_stage(spectrum, legendre, numbers, place, waves):
    slots, degrees, modes, _ = spectrum.shape
    half = legendre.shape[2]
    lats = 2 * half // waves
    rows = modes * FIELDS * PARTS
    turned = jnp.transpose(spectrum, (0, 3, 2, 1)).reshape(slots, rows, degrees)
    basis = jnp.transpose(legendre, (0, 2, 1))
    pairs = PAIRS
    chunks = degrees // CHUNK + 1
    outs = [jax.ShapeDtypeStruct((FIELDS, PARTS, lats, modes, slots), jnp.bfloat16)] * waves
    tiles = -(-rows // LANES)
    return pl.pallas_call(
        functools.partial(legendre_kernel, waves, lats, modes, pairs),
        out_shape=outs,
        grid_spec=pltpu.PrefetchScalarGridSpec(
            num_scalar_prefetch=2,
            grid=(slots // (2 * pairs),),
            in_specs=[
                pl.BlockSpec(memory_space=pl.ANY),
                pl.BlockSpec((2 * pairs, half, degrees), lambda i, *_: (i, 0, 0)),
            ],
            out_specs=[pl.BlockSpec(out.shape, lambda i, *_: (0,) * 5) for out in outs],
            scratch_shapes=[
                pltpu.VMEM((2, pairs, rows, chunks * CHUNK), jnp.bfloat16),
                pltpu.VMEM((tiles, 2 * half * slots, LANES), jnp.float32),
                pltpu.SemaphoreType.DMA((2,)),
            ],
        ),
        compiler_params=pltpu.CompilerParams(
            dimension_semantics=("arbitrary",), vmem_limit_bytes=24 << 20
        ),
        cost_estimate=cost(slots * rows * degrees * 2 * half, slots * rows * degrees),
        name="legendre_sums",
    )(numbers, place, turned, basis)


def twiddle_kernel(low_cos_ref, low_sin_ref, turn_cos_ref, turn_sin_ref, out_ref):
    slots = low_cos_ref.shape[1]
    shape = (LANES, slots)
    turn_cos = jnp.broadcast_to(turn_cos_ref[0], shape).T
    turn_sin = jnp.broadcast_to(turn_sin_ref[0], shape).T
    cos, sin = low_cos_ref[0], low_sin_ref[0]
    for block in range(out_ref.shape[3] // LANES):
        lanes = pl.ds(block * LANES, LANES)
        out_ref[0, 0, :, lanes] = cos.astype(jnp.bfloat16)
        out_ref[0, 1, :, lanes] = (-sin).astype(jnp.bfloat16)
        cos, sin = cos * turn_cos - sin * turn_sin, sin * turn_cos + cos * turn_sin


def twiddle_stage(numbers):
    waves, slots = numbers.shape
    count = NLON // 2

    def angles(residue):
        return (residue % NLON).astype(jnp.float32) * (2.0 * math.pi / NLON)

    low = angles(numbers[:, :, None] * jnp.arange(LANES, dtype=jnp.int32)[None, None, :])
    turn = angles(numbers * LANES)[:, None, :]
    weight = jnp.where(numbers == 0, 1.0, 2.0).astype(jnp.float32)[:, :, None]

    def spec(rows, last):
        return pl.BlockSpec((1, rows, last), lambda i: (i, 0, 0))

    return pl.pallas_call(
        twiddle_kernel,
        out_shape=jax.ShapeDtypeStruct((waves, PARTS, slots, count), jnp.bfloat16),
        grid=(waves,),
        in_specs=[spec(slots, LANES), spec(slots, LANES), spec(1, slots), spec(1, slots)],
        out_specs=pl.BlockSpec((1, PARTS, slots, count), lambda i: (i, 0, 0, 0)),
        compiler_params=pltpu.CompilerParams(vmem_limit_bytes=8 << 20),
        cost_estimate=cost(8 * waves * slots * count, 4 * waves * slots * count),
        name="twiddles",
    )(weight * jnp.cos(low), weight * jnp.sin(low), jnp.cos(turn), jnp.sin(turn))


def synthesis_kernel(waves, levs, field, place_ref, *refs):
    blocks, (sign_ref, twiddle_ref) = refs[:waves], refs[waves : waves + 2]
    outs, (left, grid) = refs[waves + 2 : -2], refs[-2:]
    _, _, lats, modes, slots = blocks[0].shape
    rows = lats * modes
    for d in range(waves):
        sign = sign_ref[d]
        for p in range(PARTS):
            values = blocks[d][field, p].reshape(rows, slots)
            lanes = pl.ds((d * PARTS + p) * slots, slots)
            left[:rows, lanes] = values
            left[rows:, lanes] = values * sign

    width = NLON // levs
    ratio = width // TILE
    steps = twiddle_ref.shape[3] // TILE
    lane = lax.broadcasted_iota(jnp.int32, (rows, LANES), 1)
    half = {}
    for step in range(steps):
        right = twiddle_ref[:, :, :, pl.ds(step * TILE, TILE)]
        right = right.reshape(waves * PARTS * slots, TILE)
        result = jnp.dot(left[...], right, preferred_element_type=jnp.float32)
        result = result.astype(jnp.bfloat16)
        for which in range(2):
            values = result[which * rows : (which + 1) * rows]
            owner, inner = divmod(step + which * steps, ratio)
            grid[owner, :, pl.ds(inner * TILE, TILE)] = values
            if inner == 0:
                half[owner, 0] = values[:, :LANES]
            if inner == ratio - 1:
                half[owner, 1] = values[:, -LANES:]
    for owner in range(levs):
        grid[owner, :, pl.ds(width, LANES)] = jnp.where(
            lane < LANES // 2, half[(owner + 1) % levs, 0], half[(owner - 1) % levs, 1]
        )
    place = place_ref[0]
    for e in range(levs):
        outs[e][...] = grid[place ^ e]


def synthesis_stage(blocks, sign, twiddle, place, levs, field):
    waves, _, slots, count = twiddle.shape
    _, _, lats, modes, _ = blocks[0].shape
    rows = lats * modes
    width = NLON // levs + LANES
    depth = waves * PARTS * slots
    return pl.pallas_call(
        functools.partial(synthesis_kernel, waves, levs, field),
        out_shape=[jax.ShapeDtypeStruct((rows, width), jnp.bfloat16)] * levs,
        in_specs=[pl.BlockSpec(memory_space=pltpu.SMEM)] + [vmem()] * (waves + 2),
        out_specs=[vmem()] * levs,
        scratch_shapes=[
            pltpu.VMEM((2 * rows, depth), jnp.bfloat16),
            pltpu.VMEM((levs, rows, width), jnp.bfloat16),
        ],
        compiler_params=pltpu.CompilerParams(vmem_limit_bytes=16 << 20),
        cost_estimate=cost(4 * rows * depth * count, 2 * depth * count),
        name="synthesis",
    )(place, *blocks, sign, twiddle)


def three_terms(matrix):
    high = matrix.astype(jnp.bfloat16)
    rest = matrix - high.astype(jnp.float32)
    middle = rest.astype(jnp.bfloat16)
    low = (rest - middle.astype(jnp.float32)).astype(jnp.bfloat16)
    return jnp.concatenate([high, middle, low], axis=0)


def levels_of(terms, blocks, lat, modes):
    count = terms.shape[0] // 3
    rows = jnp.concatenate(
        [block[lat * modes : (lat + 1) * modes].astype(jnp.float32) for block in blocks], axis=0
    ).astype(jnp.bfloat16)
    result = jnp.dot(terms, rows, preferred_element_type=jnp.float32)
    return result[:count] + (result[count : 2 * count] + result[2 * count :])


def keep_edges(lat, lats, values, odd, pair_ref, diagonal_ref):
    edge = values.astype(jnp.bfloat16)
    if 0 < lat < lats - 1:
        return
    takes_pair = 1 if lat == 0 else 0

    @pl.when(odd == takes_pair)
    def _():
        pair_ref[...] = edge

    @pl.when(odd != takes_pair)
    def _():
        diagonal_ref[...] = edge


def tracer_kernel(modes, odd_ref, vertical_ref, *refs):
    blocks, (field_ref, pair_ref, diagonal_ref) = refs[:-3], refs[-3:]
    terms = three_terms(vertical_ref[...])
    lats = field_ref.shape[0]
    for lat in range(lats):
        values = levels_of(terms, blocks, lat, modes)
        field_ref[lat] = values
        keep_edges(lat, lats, values, odd_ref[0], pair_ref, diagonal_ref)


def courant_kernel(modes, vertical_ref, *refs):
    blocks, field_ref = refs[:-1], refs[-1]
    terms = three_terms(vertical_ref[...])
    for lat in range(field_ref.shape[0]):
        field_ref[lat] = courant_max * jnp.tanh(levels_of(terms, blocks, lat, modes))


def upwind(center, western, eastern, northern, southern, courant_x, courant_y):
    return (
        center
        - jnp.maximum(courant_x, 0.0) * (center - western)
        - jnp.minimum(courant_x, 0.0) * (eastern - center)
        - jnp.maximum(courant_y, 0.0) * (center - northern)
        - jnp.minimum(courant_y, 0.0) * (southern - center)
    )


def stepped(lat, odd, tracer_ref, pair_ref, diagonal_ref, courant_x, courant_y):
    lats, _, width = tracer_ref.shape
    center = tracer_ref[lat]

    def outside(takes_pair):
        pair = pair_ref[...].astype(jnp.float32)
        diagonal = diagonal_ref[...].astype(jnp.float32)
        return jnp.where(odd == takes_pair, pair, diagonal)

    northern = tracer_ref[lat - 1] if lat > 0 else outside(1)
    southern = tracer_ref[lat + 1] if lat < lats - 1 else outside(0)
    return upwind(
        center,
        pltpu.roll(center, 1, 1),
        pltpu.roll(center, width - 1, 1),
        northern,
        southern,
        courant_x,
        courant_y,
    )


def first_step_kernel(modes, odd_ref, vertical_ref, tracer_ref, pair_ref, diagonal_ref, x_ref, *refs):
    blocks, (y_ref, out_ref, next_pair_ref, next_diagonal_ref) = refs[:-4], refs[-4:]
    terms = three_terms(vertical_ref[...])
    lats = tracer_ref.shape[0]
    odd = odd_ref[0]
    for lat in (0, lats - 1, *range(1, lats - 1)):
        courant_y = courant_max * jnp.tanh(levels_of(terms, blocks, lat, modes))
        y_ref[lat] = courant_y
        values = stepped(lat, odd, tracer_ref, pair_ref, diagonal_ref, x_ref[lat], courant_y)
        out_ref[lat] = values
        keep_edges(lat, lats, values, odd, next_pair_ref, next_diagonal_ref)


def second_step_kernel(odd_ref, tracer_ref, pair_ref, diagonal_ref, x_ref, y_ref, out_ref):
    width = out_ref.shape[2]
    for lat in range(tracer_ref.shape[0]):
        values = stepped(
            lat, odd_ref[0], tracer_ref, pair_ref, diagonal_ref, x_ref[lat], y_ref[lat]
        )
        out_ref[:, lat, :] = values[:, :width]


def local_call(kernel, outs, name, *operands):
    smem = pl.BlockSpec(memory_space=pltpu.SMEM)
    return pl.pallas_call(
        kernel,
        out_shape=outs,
        in_specs=[smem if operand.dtype == jnp.int32 else vmem() for operand in operands],
        out_specs=jax.tree.map(lambda _: vmem(), outs),
        compiler_params=pltpu.CompilerParams(vmem_limit_bytes=16 << 20),
        cost_estimate=cost(4_000_000, 4_000_000),
        name=name,
    )(*operands)


def exchange(blocks, axis):
    count = lax.axis_size(axis)
    return [blocks[0]] + [
        lax.ppermute(blocks[d], axis, [(i, i ^ d) for i in range(count)]) for d in range(1, count)
    ]


def edges(pair, diagonal):
    count = lax.axis_size("wave")
    steps = [(i, i + 1) for i in range(1, count - 1, 2)]
    diagonal = lax.ppermute(diagonal, "wave", steps + [(b, a) for a, b in steps])
    pair = lax.ppermute(pair, "wave", [(i, i ^ 1) for i in range(count)])
    return pair, diagonal


def tiled_body(spectrum, legendre, wave_numbers, vertical):
    waves, levs = lax.axis_size("wave"), lax.axis_size("lev")
    slots, degrees, modes, _ = spectrum.shape
    levels = vertical.shape[0]
    lats = 2 * legendre.shape[2] // waves
    width = NLON // levs
    wave_place, lev_place = lax.axis_index("wave"), lax.axis_index("lev")
    odd = lax.rem(wave_place, 2)[None]

    fourier = legendre_stage(spectrum, legendre, wave_numbers, wave_place[None], waves)
    by_wave = wave_numbers.reshape(waves, slots)[wave_place ^ jnp.arange(waves)]
    by_lev = vertical.reshape(levels, levs, modes)[:, lev_place ^ jnp.arange(levs)]
    by_lev = by_lev.reshape(levels, levs * modes)
    sign = jnp.where(by_wave % 2 == 0, 1.0, -1.0).astype(jnp.bfloat16)[:, None, :]
    twiddle = twiddle_stage(by_wave)
    received = exchange(fourier, "wave")
    columns = {}
    for field in (2, 0, 1):
        grid = synthesis_stage(received, sign, twiddle, lev_place[None], levs, field)
        columns[field] = exchange(grid, "lev")

    whole = jax.ShapeDtypeStruct((lats, levels, width + LANES), jnp.float32)
    row = jax.ShapeDtypeStruct((levels, width + LANES), jnp.bfloat16)
    tracer, pair, diagonal = local_call(
        functools.partial(tracer_kernel, modes),
        (whole, row, row),
        "tracer",
        odd,
        by_lev,
        *columns[2],
    )
    pair, diagonal = edges(pair, diagonal)
    courant_x = local_call(
        functools.partial(courant_kernel, modes), whole, "courant_x", by_lev, *columns[0]
    )
    courant_y, tracer, next_pair, next_diagonal = local_call(
        functools.partial(first_step_kernel, modes),
        (whole, whole, row, row),
        "first_step",
        odd,
        by_lev,
        tracer,
        pair,
        diagonal,
        courant_x,
        *columns[1],
    )
    pair, diagonal = edges(next_pair, next_diagonal)
    return local_call(
        second_step_kernel,
        jax.ShapeDtypeStruct((levels, lats, width), jnp.float32),
        "second_step",
        odd,
        tracer,
        pair,
        diagonal,
        courant_x,
        courant_y,
    )


def body(spectrum, legendre, wave_numbers, vertical):
    waves, levs = lax.axis_size("wave"), lax.axis_size("lev")
    slots, degrees, modes, _ = spectrum.shape
    tiled = (
        slots % LANES == 0
        and modes % 8 == 0
        and degrees % CHUNK == 0
        and waves & (waves - 1) == 0
        and levs & (levs - 1) == 0
        and NLON // levs % TILE == 0
        and levs % 2 == 0
        and 2 * legendre.shape[2] // waves >= 2
    )
    form = tiled_body if tiled else plain_body
    return form(spectrum, legendre, wave_numbers, vertical)


def solution(mesh):
    in_specs = (P("wave", None, "lev", None), P("wave", None, None), P(), P())
    out_specs = P(None, "wave", "lev")
    return jax.shard_map(body, mesh=mesh, in_specs=in_specs, out_specs=out_specs, check_vma=False)
```

```python
import functools
import math

import jax
import jax.numpy as jnp
from jax import lax
from jax.experimental import pallas as pl
from jax.experimental.pallas import tpu as pltpu
from jax.sharding import PartitionSpec as P

NLON = 2048
FIELDS = 3
PARTS = 2
LANES = 128
CHUNK = 256
TILE = 256
PAIRS = 8
GROUP = 4
AHEAD = 2

courant_max = 0.45


def padded(block, sides, width, periodic):
    for axis, dim in sides:
        count = lax.axis_size(axis)
        forward = [(i, i + 1) for i in range(count - 1)]
        if periodic:
            forward.append((count - 1, 0))
        backward = [(target, source) for source, target in forward]
        low = lax.ppermute(
            lax.slice_in_dim(block, block.shape[dim] - width, None, axis=dim), axis, forward
        )
        high = lax.ppermute(lax.slice_in_dim(block, 0, width, axis=dim), axis, backward)
        block = jnp.concatenate([low, block, high], axis=dim)
    return block


def twiddles(numbers):
    longitude = jnp.arange(NLON, dtype=jnp.int32)
    residue = numbers[:, None] * longitude[None, :] % NLON
    angles = residue.astype(jnp.float32) * (2.0 * math.pi / NLON)
    weight = jnp.where(numbers == 0, 1.0, 2.0).astype(jnp.float32)[:, None]
    return jnp.stack([weight * jnp.cos(angles), -weight * jnp.sin(angles)]).astype(jnp.bfloat16)


def parity_columns(coefficient, degree, lengths):
    counted = degree < lengths[:, None]
    even_mask = counted & (degree % 2 == 0)
    odd_mask = counted & (degree % 2 == 1)
    return jnp.concatenate(
        [
            jnp.where(even_mask[:, :, None], coefficient, 0),
            jnp.where(odd_mask[:, :, None], coefficient, 0),
        ],
        axis=2,
    )


def padded_sums(coefficient, basis, own_numbers):
    degree_count = coefficient.shape[1]
    degree = jnp.arange(degree_count, dtype=jnp.int32)[None, :]
    masked = parity_columns(coefficient, degree, degree_count - own_numbers)
    return jnp.einsum("skc,ski->sci", masked, basis, preferred_element_type=jnp.float32)


def upwind_core(extended, courant_x, courant_y):
    center = extended[:, 1:-1, 1:-1]
    western = extended[:, 1:-1, :-2]
    eastern = extended[:, 1:-1, 2:]
    northern = extended[:, :-2, 1:-1]
    southern = extended[:, 2:, 1:-1]
    return (
        center
        - jnp.maximum(courant_x, 0.0) * (center - western)
        - jnp.minimum(courant_x, 0.0) * (eastern - center)
        - jnp.maximum(courant_y, 0.0) * (center - northern)
        - jnp.minimum(courant_y, 0.0) * (southern - center)
    )


def plain_body(spectrum, legendre, wave_numbers, vertical):
    slot_count, degree_count, level_count, part_count = spectrum.shape
    columns = level_count * part_count
    coefficient = spectrum.reshape(slot_count, degree_count, columns)
    first_slot = lax.axis_index("wave") * slot_count
    own_numbers = lax.dynamic_slice_in_dim(wave_numbers, first_slot, slot_count)
    partial_sums = padded_sums(coefficient, legendre, own_numbers)
    even_sums = partial_sums[:, :columns]
    odd_sums = partial_sums[:, columns:]
    northern = even_sums + odd_sums
    southern = jnp.flip(even_sums - odd_sums, axis=2)
    fourier = jnp.concatenate([northern, southern], axis=2).astype(jnp.bfloat16)
    received = lax.all_to_all(fourier, "wave", split_axis=2, concat_axis=0, tiled=True)
    lat_count = received.shape[2]
    received = received.reshape(received.shape[0], level_count, FIELDS, PARTS, lat_count)
    twiddle = twiddles(wave_numbers)
    grid_values = jnp.einsum(
        "smfrl,rsj->lmfj", received, twiddle, preferred_element_type=jnp.float32
    ).astype(jnp.bfloat16)
    column_values = lax.all_to_all(grid_values, "lev", split_axis=3, concat_axis=1, tiled=True)
    fields = jnp.einsum(
        "vm,lmfj->fvlj",
        vertical,
        column_values.astype(jnp.float32),
        precision=lax.Precision.HIGHEST,
    )
    courant_x = courant_max * jnp.tanh(fields[0])
    courant_y = courant_max * jnp.tanh(fields[1])
    tracer = fields[2]
    for sweep in range(2):
        extended = padded(tracer, (("wave", 1),), 1, False)
        extended = padded(extended, (("lev", 2),), 1, True)
        tracer = upwind_core(extended, courant_x, courant_y)
    return tracer


def vmem():
    return pl.BlockSpec(memory_space=pltpu.VMEM)


def cost(flops, count_bytes):
    return pl.CostEstimate(flops=flops, bytes_accessed=count_bytes, transcendentals=0)


def legendre_kernel(numbers_ref, place_ref, spectrum_ref, legendre_ref, *refs):
    outs, (held, basis_held, order, sums, arrived) = refs[:-5], refs[-5:]
    waves = len(outs)
    _, _, lats, modes, _ = outs[0].shape
    buffers, pairs, rows, _ = held.shape
    slots, half, degrees = legendre_ref.shape
    chunks = degrees // CHUNK + 1
    steps = slots // (2 * pairs)
    ahead = buffers - 1
    place = place_ref[0]
    many = 2 * GROUP

    def plan(index):
        first = degrees - numbers_ref[place * slots + 2 * index]
        second = degrees - numbers_ref[place * slots + 2 * index + 1]
        return first, second, lax.shift_right_logical(first + (CHUNK - 1), CHUNK.bit_length() - 1)

    def fetch(group, slot):
        pltpu.make_async_copy(
            legendre_ref.at[pl.ds(group * 2 * pairs, 2 * pairs)],
            basis_held.at[slot],
            arrived.at[slot],
        ).start()
        for pair in range(pairs):
            index = group * pairs + pair
            _, _, edge = plan(index)
            for t in range(chunks):
                inside = t < edge
                source = jnp.where(inside, 2 * index, 2 * index + 1)
                block = jnp.where(inside, t, t - edge)
                start = pl.multiple_of(block * CHUNK, CHUNK)
                pltpu.make_async_copy(
                    spectrum_ref.at[source, :, pl.ds(start, CHUNK)],
                    held.at[slot, pair, :, pl.ds(t * CHUNK, CHUNK)],
                    arrived.at[slot],
                ).start()

    for group in range(min(ahead, steps)):
        fetch(group, group)

    row = lax.broadcasted_iota(jnp.int32, order.shape, 0)
    column = lax.broadcasted_iota(jnp.int32, order.shape, 1)
    wanted = lax.rem(row, many) * (2 * half) + lax.div(row, many)
    order[...] = jnp.where(column == wanted, 1.0, 0.0).astype(jnp.bfloat16)

    def work(step, fetches):
        now = lax.rem(step, buffers)
        for buffer in (held, basis_held):
            pltpu.make_async_copy(buffer.at[now], buffer.at[now], arrived.at[now]).wait()
        if fetches:
            fetch(step + ahead, lax.rem(step + ahead, buffers))
        lane = lax.broadcasted_iota(jnp.int32, (half, CHUNK), 1)
        sign = jnp.where(lane % 2 == 0, 1.0, -1.0)
        results = []
        for pair in range(pairs):
            index = step * pairs + pair
            first, second, edge = plan(index)
            columns = []
            for t in range(chunks):
                inside = t < edge
                local = jnp.where(inside, 2 * pair, 2 * pair + 1)
                block = jnp.where(inside, t, t - edge)
                start = pl.multiple_of(block * CHUNK, CHUNK)
                length = jnp.where(inside, first, second) - start
                values = basis_held[now, local, :, pl.ds(start, CHUNK)].astype(jnp.float32)
                values = jnp.where(lane < length, values, 0.0)
                north_first = values * jnp.where(inside, 1.0, 0.0)
                north_second = values - north_first
                parts = [north_first, north_first * sign, north_second, north_second * sign]
                columns.append(jnp.concatenate(parts, axis=0).astype(jnp.bfloat16))
            result = lax.dot_general(
                jnp.concatenate(columns, axis=1),
                held[now, pair],
                (((1,), (1,)), ((), ())),
                preferred_element_type=jnp.float32,
            )
            results.append(result.astype(jnp.bfloat16))
            if len(results) == GROUP:
                slot = pl.multiple_of(2 * (index - (GROUP - 1)), many)
                ordered = jnp.dot(
                    order[...], jnp.concatenate(results, axis=0), preferred_element_type=jnp.float32
                )
                results = []
                for low in range(0, rows, LANES):
                    width = min(LANES, rows - low)
                    part = ordered[:, low : low + width].reshape(2 * half, many, width)
                    sums[low // LANES, :, pl.ds(slot, many), :width] = part

    lax.fori_loop(0, steps - ahead, lambda step, _: work(step, True), None)
    lax.fori_loop(steps - ahead, steps, lambda step, _: work(step, False), None)

    for d in range(waves):
        for l in range(lats):
            lat = (place ^ d) * lats + l
            row = jnp.where(lat < half, lat, 3 * half - 1 - lat)
            turned = [
                sums[low // LANES, row].T.astype(jnp.bfloat16) for low in range(0, rows, LANES)
            ]
            whole = jnp.concatenate(turned, axis=0)
            for f in range(FIELDS):
                for p in range(PARTS):
                    base = (f * PARTS + p) * modes
                    outs[d][f, p, l] = whole[base : base + modes]


def legendre_stage(spectrum, legendre, numbers, place, waves):
    slots, degrees, modes, _ = spectrum.shape
    half = legendre.shape[2]
    lats = 2 * half // waves
    rows = modes * FIELDS * PARTS
    turned = jnp.transpose(spectrum, (0, 3, 2, 1)).reshape(slots, rows, degrees)
    basis = jnp.transpose(legendre, (0, 2, 1))
    chunks = degrees // CHUNK + 1
    tiles = -(-rows // LANES)
    smem = pl.BlockSpec(memory_space=pltpu.SMEM)
    away = pl.BlockSpec(memory_space=pl.ANY)
    return pl.pallas_call(
        legendre_kernel,
        out_shape=[jax.ShapeDtypeStruct((FIELDS, PARTS, lats, modes, slots), jnp.bfloat16)] * waves,
        in_specs=[smem, smem, away, away],
        out_specs=[vmem()] * waves,
        scratch_shapes=[
            pltpu.VMEM((AHEAD + 1, PAIRS, rows, chunks * CHUNK), jnp.bfloat16),
            pltpu.VMEM((AHEAD + 1, 2 * PAIRS, half, degrees), jnp.bfloat16),
            pltpu.VMEM((GROUP * 4 * half, GROUP * 4 * half), jnp.bfloat16),
            pltpu.VMEM((tiles, 2 * half, slots, LANES), jnp.float32),
            pltpu.SemaphoreType.DMA((AHEAD + 1,)),
        ],
        compiler_params=pltpu.CompilerParams(vmem_limit_bytes=58 << 20),
        cost_estimate=cost(slots * rows * degrees * 2 * half, slots * rows * degrees),
        name="legendre_sums",
    )(numbers, place, turned, basis)


def twiddle_kernel(place_ref, low_cos_ref, low_sin_ref, turn_cos_ref, turn_sin_ref, out_ref):
    slots = low_cos_ref.shape[1]
    shape = (LANES, slots)
    turn_cos = jnp.broadcast_to(turn_cos_ref[0], shape).T
    turn_sin = jnp.broadcast_to(turn_sin_ref[0], shape).T
    cos, sin = low_cos_ref[0], low_sin_ref[0]
    for block in range(out_ref.shape[3] // LANES):
        lanes = pl.ds(block * LANES, LANES)
        out_ref[0, 0, :, lanes] = cos.astype(jnp.bfloat16)
        out_ref[0, 1, :, lanes] = (-sin).astype(jnp.bfloat16)
        cos, sin = cos * turn_cos - sin * turn_sin, sin * turn_cos + cos * turn_sin


def twiddle_stage(numbers, place):
    waves, slots = numbers.shape
    count = NLON // 2

    def angles(residue):
        return (residue % NLON).astype(jnp.float32) * (2.0 * math.pi / NLON)

    low = angles(numbers[:, :, None] * jnp.arange(LANES, dtype=jnp.int32)[None, None, :])
    turn = angles(numbers * LANES)[:, None, :]
    weight = jnp.where(numbers == 0, 1.0, 2.0).astype(jnp.float32)[:, :, None]

    def spec(rows, last):
        return pl.BlockSpec((1, rows, last), lambda i, place_ref: (place_ref[0] ^ i, 0, 0))

    return pl.pallas_call(
        twiddle_kernel,
        out_shape=jax.ShapeDtypeStruct((waves, PARTS, slots, count), jnp.bfloat16),
        grid_spec=pltpu.PrefetchScalarGridSpec(
            num_scalar_prefetch=1,
            grid=(waves,),
            in_specs=[spec(slots, LANES), spec(slots, LANES), spec(1, slots), spec(1, slots)],
            out_specs=pl.BlockSpec((1, PARTS, slots, count), lambda i, _: (i, 0, 0, 0)),
        ),
        compiler_params=pltpu.CompilerParams(vmem_limit_bytes=8 << 20),
        cost_estimate=cost(8 * waves * slots * count, 4 * waves * slots * count),
        name="twiddles",
    )(place, weight * jnp.cos(low), weight * jnp.sin(low), jnp.cos(turn), jnp.sin(turn))


def synthesis_kernel(waves, levs, fields, wave_ref, lev_ref, *refs):
    blocks, (sign_ref, twiddle_ref) = refs[:waves], refs[waves : waves + 2]
    outs, (left, grid) = refs[waves + 2 : -2], refs[-2:]
    _, _, lats, modes, slots = blocks[0].shape
    each = lats * modes
    rows = each * len(fields)
    for d in range(waves):
        sign = sign_ref[wave_ref[0] ^ d]
        for p in range(PARTS):
            lanes = pl.ds((d * PARTS + p) * slots, slots)
            for place, field in enumerate(fields):
                values = blocks[d][field, p].reshape(each, slots)
                left[place * each : (place + 1) * each, lanes] = values
                left[rows + place * each : rows + (place + 1) * each, lanes] = values * sign

    width = NLON // levs
    ratio = width // TILE
    steps = twiddle_ref.shape[3] // TILE
    lane = lax.broadcasted_iota(jnp.int32, (rows, LANES), 1)
    for step in range(steps):
        right = twiddle_ref[:, :, :, pl.ds(step * TILE, TILE)]
        right = right.reshape(waves * PARTS * slots, TILE)
        result = jnp.dot(left[...], right, preferred_element_type=jnp.float32)
        result = result.astype(jnp.bfloat16)
        for which in range(2):
            owner, inner = divmod(step + which * steps, ratio)
            grid[owner, :, pl.ds(inner * TILE, TILE)] = result[which * rows : (which + 1) * rows]
    for owner in range(levs):
        grid[owner, :, pl.ds(width, LANES)] = jnp.where(
            lane < LANES // 2,
            grid[(owner + 1) % levs, :, :LANES],
            grid[(owner - 1) % levs, :, pl.ds(width - LANES, LANES)],
        )
    place = lev_ref[0]
    for e in range(levs):
        outs[e][...] = grid[place ^ e]


def synthesis_stage(blocks, sign, twiddle, wave_place, lev_place, levs, fields):
    waves, _, slots, count = twiddle.shape
    _, _, lats, modes, _ = blocks[0].shape
    rows = lats * modes * len(fields)
    width = NLON // levs + LANES
    depth = waves * PARTS * slots
    return pl.pallas_call(
        functools.partial(synthesis_kernel, waves, levs, fields),
        out_shape=[jax.ShapeDtypeStruct((rows, width), jnp.bfloat16)] * levs,
        in_specs=[pl.BlockSpec(memory_space=pltpu.SMEM)] * 2 + [vmem()] * (waves + 2),
        out_specs=[vmem()] * levs,
        scratch_shapes=[
            pltpu.VMEM((2 * rows, depth), jnp.bfloat16),
            pltpu.VMEM((levs, rows, width), jnp.bfloat16),
        ],
        compiler_params=pltpu.CompilerParams(vmem_limit_bytes=12 << 20),
        cost_estimate=cost(4 * rows * depth * count, 2 * depth * count),
        name="synthesis",
    )(wave_place, lev_place, *blocks, sign, twiddle)


def three_terms(matrix):
    high = matrix.astype(jnp.bfloat16)
    rest = matrix - high.astype(jnp.float32)
    middle = rest.astype(jnp.bfloat16)
    low = (rest - middle.astype(jnp.float32)).astype(jnp.bfloat16)
    return jnp.concatenate([high, middle, low], axis=0)


def levels_of(terms, place, blocks, gathered, base, modes):
    count = terms.shape[0] // 3
    for e, block in enumerate(blocks):
        start = pl.multiple_of((place ^ e) * modes, modes)
        gathered[pl.ds(start, modes)] = block[base : base + modes].astype(jnp.float32)
    rows = gathered[...].astype(jnp.bfloat16)
    result = jnp.dot(terms, rows, preferred_element_type=jnp.float32)
    return result[:count] + (result[count : 2 * count] + result[2 * count :])


def keep_edges(lat, lats, values, odd, pair_ref, diagonal_ref):
    edge = values.astype(jnp.bfloat16)
    if 0 < lat < lats - 1:
        return
    takes_pair = 1 if lat == 0 else 0

    @pl.when(odd == takes_pair)
    def _():
        pair_ref[...] = edge

    @pl.when(odd != takes_pair)
    def _():
        diagonal_ref[...] = edge


def tracer_kernel(modes, odd_ref, lev_ref, vertical_ref, *refs):
    blocks, (field_ref, pair_ref, diagonal_ref, gathered) = refs[:-4], refs[-4:]
    terms = three_terms(vertical_ref[...])
    lats = field_ref.shape[0]
    for lat in range(lats):
        values = levels_of(terms, lev_ref[0], blocks, gathered, lat * modes, modes)
        field_ref[lat] = values
        keep_edges(lat, lats, values, odd_ref[0], pair_ref, diagonal_ref)


def upwind(center, western, eastern, northern, southern, courant_x, courant_y):
    return (
        center
        - jnp.maximum(courant_x, 0.0) * (center - western)
        - jnp.minimum(courant_x, 0.0) * (eastern - center)
        - jnp.maximum(courant_y, 0.0) * (center - northern)
        - jnp.minimum(courant_y, 0.0) * (southern - center)
    )


def stepped(lat, odd_ref, end_ref, tracer_ref, pair_ref, diagonal_ref, courant_x, courant_y):
    lats, _, width = tracer_ref.shape
    center = tracer_ref[lat]

    def outside(takes_pair):
        pair = pair_ref[...].astype(jnp.float32)
        diagonal = jnp.where(end_ref[0] == 1, 0.0, diagonal_ref[...].astype(jnp.float32))
        return jnp.where(odd_ref[0] == takes_pair, pair, diagonal)

    northern = tracer_ref[lat - 1] if lat > 0 else outside(1)
    southern = tracer_ref[lat + 1] if lat < lats - 1 else outside(0)
    return upwind(
        center,
        pltpu.roll(center, 1, 1),
        pltpu.roll(center, width - 1, 1),
        northern,
        southern,
        courant_x,
        courant_y,
    )


def first_step_kernel(
    modes, odd_ref, end_ref, lev_ref, vertical_ref, tracer_ref, pair_ref, diagonal_ref, *refs
):
    blocks, (x_ref, y_ref, out_ref, next_pair_ref, next_diagonal_ref, gathered) = refs[:-6], refs[-6:]
    terms = three_terms(vertical_ref[...])
    lats = tracer_ref.shape[0]

    def courant(field, lat):
        base = (field * lats + lat) * modes
        velocity = levels_of(terms, lev_ref[0], blocks, gathered.at[field], base, modes)
        return courant_max * jnp.tanh(velocity)

    for lat in (0, lats - 1, *range(1, lats - 1)):
        courant_x, courant_y = courant(0, lat), courant(1, lat)
        x_ref[lat] = courant_x
        y_ref[lat] = courant_y
        values = stepped(
            lat, odd_ref, end_ref, tracer_ref, pair_ref, diagonal_ref, courant_x, courant_y
        )
        out_ref[lat] = values
        keep_edges(lat, lats, values, odd_ref[0], next_pair_ref, next_diagonal_ref)


def second_step_kernel(odd_ref, end_ref, tracer_ref, pair_ref, diagonal_ref, x_ref, y_ref, out_ref):
    width = out_ref.shape[2]
    for lat in range(tracer_ref.shape[0]):
        values = stepped(
            lat, odd_ref, end_ref, tracer_ref, pair_ref, diagonal_ref, x_ref[lat], y_ref[lat]
        )
        out_ref[:, lat, :] = values[:, :width]


def local_call(kernel, outs, scratch, name, *operands):
    smem = pl.BlockSpec(memory_space=pltpu.SMEM)
    return pl.pallas_call(
        kernel,
        out_shape=outs,
        in_specs=[smem if operand.dtype == jnp.int32 else vmem() for operand in operands],
        out_specs=jax.tree.map(lambda _: vmem(), outs),
        scratch_shapes=scratch,
        compiler_params=pltpu.CompilerParams(vmem_limit_bytes=16 << 20),
        cost_estimate=cost(4_000_000, 4_000_000),
        name=name,
    )(*operands)


def exchange(blocks, axis):
    count = lax.axis_size(axis)
    return [blocks[0]] + [
        lax.ppermute(blocks[d], axis, [(i, i ^ d) for i in range(count)]) for d in range(1, count)
    ]


def edges(pair, diagonal):
    count = lax.axis_size("wave")
    steps = [(i, i + 1) for i in range(1, count - 1, 2)] + [(0, 0)]
    steps = steps + [(b, a) for a, b in steps[:-1]] + [(count - 1, count - 1)]
    diagonal = lax.ppermute(diagonal, "wave", steps)
    pair = lax.ppermute(pair, "wave", [(i, i ^ 1) for i in range(count)])
    return pair, diagonal


def tiled_body(spectrum, legendre, wave_numbers, vertical):
    waves, levs = lax.axis_size("wave"), lax.axis_size("lev")
    slots, degrees, modes, _ = spectrum.shape
    levels = vertical.shape[0]
    lats = 2 * legendre.shape[2] // waves
    width = NLON // levs
    wave_place, lev_place = lax.axis_index("wave"), lax.axis_index("lev")
    at_end = (wave_place == 0) | (wave_place == waves - 1)
    odd, at_end = lax.rem(wave_place, 2)[None], at_end.astype(jnp.int32)[None]
    wave_place, lev_place = wave_place[None], lev_place[None]

    fourier = legendre_stage(spectrum, legendre, wave_numbers, wave_place, waves)
    by_wave = wave_numbers.reshape(waves, slots)
    sign = jnp.where(by_wave % 2 == 0, 1.0, -1.0).astype(jnp.bfloat16)[:, None, :]
    twiddle = twiddle_stage(by_wave, wave_place)
    received = exchange(fourier, "wave")
    columns = [
        exchange(
            synthesis_stage(received, sign, twiddle, wave_place, lev_place, levs, fields), "lev"
        )
        for fields in ((2,), (0, 1))
    ]

    whole = jax.ShapeDtypeStruct((lats, levels, width + LANES), jnp.float32)
    row = jax.ShapeDtypeStruct((levels, width + LANES), jnp.bfloat16)
    gathered = (levs * modes, width + LANES)
    tracer, pair, diagonal = local_call(
        functools.partial(tracer_kernel, modes),
        (whole, row, row),
        [pltpu.VMEM(gathered, jnp.float32)],
        "tracer",
        odd,
        lev_place,
        vertical,
        *columns[0],
    )
    pair, diagonal = edges(pair, diagonal)
    courant_x, courant_y, tracer, next_pair, next_diagonal = local_call(
        functools.partial(first_step_kernel, modes),
        (whole, whole, whole, row, row),
        [pltpu.VMEM((2, *gathered), jnp.float32)],
        "first_step",
        odd,
        at_end,
        lev_place,
        vertical,
        tracer,
        pair,
        diagonal,
        *columns[1],
    )
    pair, diagonal = edges(next_pair, next_diagonal)
    return local_call(
        second_step_kernel,
        jax.ShapeDtypeStruct((levels, lats, width), jnp.float32),
        [],
        "second_step",
        odd,
        at_end,
        tracer,
        pair,
        diagonal,
        courant_x,
        courant_y,
    )


def body(spectrum, legendre, wave_numbers, vertical):
    waves, levs = lax.axis_size("wave"), lax.axis_size("lev")
    slots, degrees, modes, _ = spectrum.shape
    tiled = (
        slots % LANES == 0
        and slots % (2 * PAIRS) == 0
        and slots > 2 * PAIRS * AHEAD
        and legendre.shape[2] % 16 == 0
        and modes % 8 == 0
        and degrees % CHUNK == 0
        and waves & (waves - 1) == 0
        and levs & (levs - 1) == 0
        and NLON // levs % TILE == 0
        and levs % 2 == 0
        and 2 * legendre.shape[2] // waves >= 2
    )
    form = tiled_body if tiled else plain_body
    return form(spectrum, legendre, wave_numbers, vertical)


def solution(mesh):
    in_specs = (P("wave", None, "lev", None), P("wave", None, None), P(), P())
    out_specs = P(None, "wave", "lev")
    return jax.shard_map(body, mesh=mesh, in_specs=in_specs, out_specs=out_specs, check_vma=False)
```

```python
import functools
import math

import jax
import jax.numpy as jnp
from jax import lax
from jax.experimental import pallas as pl
from jax.experimental.pallas import tpu as pltpu
from jax.sharding import PartitionSpec as P

NLON = 2048
FIELDS = 3
PARTS = 2
LANES = 128
CHUNK = 256
TILE = 256
PAIRS = 8
GROUP = 4
AHEAD = 2

courant_max = 0.45


def padded(block, sides, width, periodic):
    for axis, dim in sides:
        count = lax.axis_size(axis)
        forward = [(i, i + 1) for i in range(count - 1)]
        if periodic:
            forward.append((count - 1, 0))
        backward = [(target, source) for source, target in forward]
        low = lax.ppermute(
            lax.slice_in_dim(block, block.shape[dim] - width, None, axis=dim), axis, forward
        )
        high = lax.ppermute(lax.slice_in_dim(block, 0, width, axis=dim), axis, backward)
        block = jnp.concatenate([low, block, high], axis=dim)
    return block


def twiddles(numbers):
    longitude = jnp.arange(NLON, dtype=jnp.int32)
    residue = numbers[:, None] * longitude[None, :] % NLON
    angles = residue.astype(jnp.float32) * (2.0 * math.pi / NLON)
    weight = jnp.where(numbers == 0, 1.0, 2.0).astype(jnp.float32)[:, None]
    return jnp.stack([weight * jnp.cos(angles), -weight * jnp.sin(angles)]).astype(jnp.bfloat16)


def parity_columns(coefficient, degree, lengths):
    counted = degree < lengths[:, None]
    even_mask = counted & (degree % 2 == 0)
    odd_mask = counted & (degree % 2 == 1)
    return jnp.concatenate(
        [
            jnp.where(even_mask[:, :, None], coefficient, 0),
            jnp.where(odd_mask[:, :, None], coefficient, 0),
        ],
        axis=2,
    )


def padded_sums(coefficient, basis, own_numbers):
    degree_count = coefficient.shape[1]
    degree = jnp.arange(degree_count, dtype=jnp.int32)[None, :]
    masked = parity_columns(coefficient, degree, degree_count - own_numbers)
    return jnp.einsum("skc,ski->sci", masked, basis, preferred_element_type=jnp.float32)


def upwind_core(extended, courant_x, courant_y):
    center = extended[:, 1:-1, 1:-1]
    western = extended[:, 1:-1, :-2]
    eastern = extended[:, 1:-1, 2:]
    northern = extended[:, :-2, 1:-1]
    southern = extended[:, 2:, 1:-1]
    return (
        center
        - jnp.maximum(courant_x, 0.0) * (center - western)
        - jnp.minimum(courant_x, 0.0) * (eastern - center)
        - jnp.maximum(courant_y, 0.0) * (center - northern)
        - jnp.minimum(courant_y, 0.0) * (southern - center)
    )


def plain_body(spectrum, legendre, wave_numbers, vertical):
    slot_count, degree_count, level_count, part_count = spectrum.shape
    columns = level_count * part_count
    coefficient = spectrum.reshape(slot_count, degree_count, columns)
    first_slot = lax.axis_index("wave") * slot_count
    own_numbers = lax.dynamic_slice_in_dim(wave_numbers, first_slot, slot_count)
    partial_sums = padded_sums(coefficient, legendre, own_numbers)
    even_sums = partial_sums[:, :columns]
    odd_sums = partial_sums[:, columns:]
    northern = even_sums + odd_sums
    southern = jnp.flip(even_sums - odd_sums, axis=2)
    fourier = jnp.concatenate([northern, southern], axis=2).astype(jnp.bfloat16)
    received = lax.all_to_all(fourier, "wave", split_axis=2, concat_axis=0, tiled=True)
    lat_count = received.shape[2]
    received = received.reshape(received.shape[0], level_count, FIELDS, PARTS, lat_count)
    twiddle = twiddles(wave_numbers)
    grid_values = jnp.einsum(
        "smfrl,rsj->lmfj", received, twiddle, preferred_element_type=jnp.float32
    ).astype(jnp.bfloat16)
    column_values = lax.all_to_all(grid_values, "lev", split_axis=3, concat_axis=1, tiled=True)
    fields = jnp.einsum(
        "vm,lmfj->fvlj",
        vertical,
        column_values.astype(jnp.float32),
        precision=lax.Precision.HIGHEST,
    )
    courant_x = courant_max * jnp.tanh(fields[0])
    courant_y = courant_max * jnp.tanh(fields[1])
    tracer = fields[2]
    for _ in range(2):
        extended = padded(tracer, (("wave", 1),), 1, False)
        extended = padded(extended, (("lev", 2),), 1, True)
        tracer = upwind_core(extended, courant_x, courant_y)
    return tracer


def vmem():
    return pl.BlockSpec(memory_space=pltpu.VMEM)


def cost(flops, count_bytes):
    return pl.CostEstimate(flops=flops, bytes_accessed=count_bytes, transcendentals=0)


def legendre_kernel(numbers_ref, place_ref, spectrum_ref, legendre_ref, *refs):
    outs, (held, basis_held, order, sums, arrived) = refs[:-5], refs[-5:]
    waves = len(outs)
    _, _, lats, modes, _ = outs[0].shape
    buffers, pairs, rows, _ = held.shape
    slots, half, degrees = legendre_ref.shape
    chunks = degrees // CHUNK + 1
    steps = slots // (2 * pairs)
    ahead = buffers - 1
    place = place_ref[0]
    many = 2 * GROUP

    def plan(index):
        first = degrees - numbers_ref[place * slots + 2 * index]
        second = degrees - numbers_ref[place * slots + 2 * index + 1]
        return first, second, lax.shift_right_logical(first + (CHUNK - 1), CHUNK.bit_length() - 1)

    def fetch(group, slot):
        pltpu.make_async_copy(
            legendre_ref.at[pl.ds(group * 2 * pairs, 2 * pairs)],
            basis_held.at[slot],
            arrived.at[slot],
        ).start()
        for pair in range(pairs):
            index = group * pairs + pair
            _, _, edge = plan(index)
            for t in range(chunks):
                inside = t < edge
                source = jnp.where(inside, 2 * index, 2 * index + 1)
                block = jnp.where(inside, t, t - edge)
                start = pl.multiple_of(block * CHUNK, CHUNK)
                pltpu.make_async_copy(
                    spectrum_ref.at[source, :, pl.ds(start, CHUNK)],
                    held.at[slot, pair, :, pl.ds(t * CHUNK, CHUNK)],
                    arrived.at[slot],
                ).start()

    for group in range(min(ahead, steps)):
        fetch(group, group)

    row = lax.broadcasted_iota(jnp.int32, order.shape, 0)
    column = lax.broadcasted_iota(jnp.int32, order.shape, 1)
    wanted = lax.rem(row, many) * (2 * half) + lax.div(row, many)
    order[...] = jnp.where(column == wanted, 1.0, 0.0).astype(jnp.bfloat16)

    def work(step, fetches):
        now = lax.rem(step, buffers)
        for buffer in (held, basis_held):
            pltpu.make_async_copy(buffer.at[now], buffer.at[now], arrived.at[now]).wait()
        if fetches:
            fetch(step + ahead, lax.rem(step + ahead, buffers))
        lane = lax.broadcasted_iota(jnp.int32, (half, CHUNK), 1)
        sign = jnp.where(lane % 2 == 0, 1.0, -1.0)
        results = []
        for pair in range(pairs):
            index = step * pairs + pair
            first, second, edge = plan(index)
            columns = []
            for t in range(chunks):
                inside = t < edge
                local = jnp.where(inside, 2 * pair, 2 * pair + 1)
                block = jnp.where(inside, t, t - edge)
                start = pl.multiple_of(block * CHUNK, CHUNK)
                length = jnp.where(inside, first, second) - start
                values = basis_held[now, local, :, pl.ds(start, CHUNK)].astype(jnp.float32)
                values = jnp.where(lane < length, values, 0.0)
                north_first = values * jnp.where(inside, 1.0, 0.0)
                north_second = values - north_first
                parts = [north_first, north_first * sign, north_second, north_second * sign]
                columns.append(jnp.concatenate(parts, axis=0).astype(jnp.bfloat16))
            result = lax.dot_general(
                jnp.concatenate(columns, axis=1),
                held[now, pair],
                (((1,), (1,)), ((), ())),
                preferred_element_type=jnp.float32,
            )
            results.append(result.astype(jnp.bfloat16))
            if len(results) == GROUP:
                slot = pl.multiple_of(2 * (index - (GROUP - 1)), many)
                ordered = jnp.dot(
                    order[...], jnp.concatenate(results, axis=0), preferred_element_type=jnp.float32
                )
                results = []
                for low in range(0, rows, LANES):
                    width = min(LANES, rows - low)
                    part = ordered[:, low : low + width].reshape(2 * half, many, width)
                    sums[low // LANES, :, pl.ds(slot, many), :width] = part

    lax.fori_loop(0, steps - ahead, lambda step, _: work(step, True), None)
    lax.fori_loop(steps - ahead, steps, lambda step, _: work(step, False), None)

    for d in range(waves):
        for l in range(lats):
            lat = (place ^ d) * lats + l
            row = jnp.where(lat < half, lat, 3 * half - 1 - lat)
            turned = [
                sums[low // LANES, row].T.astype(jnp.bfloat16) for low in range(0, rows, LANES)
            ]
            whole = jnp.concatenate(turned, axis=0)
            for f in range(FIELDS):
                for p in range(PARTS):
                    base = (f * PARTS + p) * modes
                    outs[d][f, p, l] = whole[base : base + modes]


def legendre_stage(spectrum, legendre, numbers, place, waves):
    slots, degrees, modes, _ = spectrum.shape
    half = legendre.shape[2]
    lats = 2 * half // waves
    rows = modes * FIELDS * PARTS
    turned = jnp.transpose(spectrum, (0, 3, 2, 1)).reshape(slots, rows, degrees)
    basis = jnp.transpose(legendre, (0, 2, 1))
    chunks = degrees // CHUNK + 1
    tiles = -(-rows // LANES)
    smem = pl.BlockSpec(memory_space=pltpu.SMEM)
    away = pl.BlockSpec(memory_space=pl.ANY)
    return pl.pallas_call(
        legendre_kernel,
        out_shape=[jax.ShapeDtypeStruct((FIELDS, PARTS, lats, modes, slots), jnp.bfloat16)] * waves,
        in_specs=[smem, smem, away, away],
        out_specs=[vmem()] * waves,
        scratch_shapes=[
            pltpu.VMEM((AHEAD + 1, PAIRS, rows, chunks * CHUNK), jnp.bfloat16),
            pltpu.VMEM((AHEAD + 1, 2 * PAIRS, half, degrees), jnp.bfloat16),
            pltpu.VMEM((GROUP * 4 * half, GROUP * 4 * half), jnp.bfloat16),
            pltpu.VMEM((tiles, 2 * half, slots, LANES), jnp.float32),
            pltpu.SemaphoreType.DMA((AHEAD + 1,)),
        ],
        compiler_params=pltpu.CompilerParams(vmem_limit_bytes=58 << 20),
        cost_estimate=cost(slots * rows * degrees * 2 * half, slots * rows * degrees),
        name="legendre_sums",
    )(numbers, place, turned, basis)


def twiddle_kernel(place_ref, low_cos_ref, low_sin_ref, turn_cos_ref, turn_sin_ref, out_ref):
    slots = low_cos_ref.shape[1]
    shape = (LANES, slots)
    turn_cos = jnp.broadcast_to(turn_cos_ref[0], shape).T
    turn_sin = jnp.broadcast_to(turn_sin_ref[0], shape).T
    cos, sin = low_cos_ref[0], low_sin_ref[0]
    for block in range(out_ref.shape[3] // LANES):
        lanes = pl.ds(block * LANES, LANES)
        out_ref[0, 0, :, lanes] = cos.astype(jnp.bfloat16)
        out_ref[0, 1, :, lanes] = (-sin).astype(jnp.bfloat16)
        cos, sin = cos * turn_cos - sin * turn_sin, sin * turn_cos + cos * turn_sin


def twiddle_stage(numbers, place):
    waves, slots = numbers.shape
    count = NLON // 2

    def angles(residue):
        return (residue % NLON).astype(jnp.float32) * (2.0 * math.pi / NLON)

    low = angles(numbers[:, :, None] * jnp.arange(LANES, dtype=jnp.int32)[None, None, :])
    turn = angles(numbers * LANES)[:, None, :]
    weight = jnp.where(numbers == 0, 1.0, 2.0).astype(jnp.float32)[:, :, None]

    def spec(rows, last):
        return pl.BlockSpec((1, rows, last), lambda i, place_ref: (place_ref[0] ^ i, 0, 0))

    return pl.pallas_call(
        twiddle_kernel,
        out_shape=jax.ShapeDtypeStruct((waves, PARTS, slots, count), jnp.bfloat16),
        grid_spec=pltpu.PrefetchScalarGridSpec(
            num_scalar_prefetch=1,
            grid=(waves,),
            in_specs=[spec(slots, LANES), spec(slots, LANES), spec(1, slots), spec(1, slots)],
            out_specs=pl.BlockSpec((1, PARTS, slots, count), lambda i, _: (i, 0, 0, 0)),
        ),
        compiler_params=pltpu.CompilerParams(vmem_limit_bytes=8 << 20),
        cost_estimate=cost(8 * waves * slots * count, 4 * waves * slots * count),
        name="twiddles",
    )(place, weight * jnp.cos(low), weight * jnp.sin(low), jnp.cos(turn), jnp.sin(turn))


def synthesis_kernel(waves, levs, fields, wave_ref, lev_ref, *refs):
    blocks, (sign_ref, twiddle_ref) = refs[:waves], refs[waves : waves + 2]
    outs, (left, grid) = refs[waves + 2 : -2], refs[-2:]
    _, _, lats, modes, slots = blocks[0].shape
    each = lats * modes
    rows = each * len(fields)
    for d in range(waves):
        sign = sign_ref[wave_ref[0] ^ d]
        for p in range(PARTS):
            lanes = pl.ds((d * PARTS + p) * slots, slots)
            for place, field in enumerate(fields):
                values = blocks[d][field, p].reshape(each, slots)
                left[place * each : (place + 1) * each, lanes] = values
                left[rows + place * each : rows + (place + 1) * each, lanes] = values * sign

    width = NLON // levs
    ratio = width // TILE
    steps = twiddle_ref.shape[3] // TILE
    lane = lax.broadcasted_iota(jnp.int32, (rows, LANES), 1)
    for step in range(steps):
        right = twiddle_ref[:, :, :, pl.ds(step * TILE, TILE)]
        right = right.reshape(waves * PARTS * slots, TILE)
        result = jnp.dot(left[...], right, preferred_element_type=jnp.float32)
        result = result.astype(jnp.bfloat16)
        for which in range(2):
            owner, inner = divmod(step + which * steps, ratio)
            grid[owner, :, pl.ds(inner * TILE, TILE)] = result[which * rows : (which + 1) * rows]
    for owner in range(levs):
        grid[owner, :, pl.ds(width, LANES)] = jnp.where(
            lane < LANES // 2,
            grid[(owner + 1) % levs, :, :LANES],
            grid[(owner - 1) % levs, :, pl.ds(width - LANES, LANES)],
        )
    place = lev_ref[0]
    for e in range(levs):
        outs[e][...] = grid[place ^ e]


def synthesis_stage(blocks, sign, twiddle, wave_place, lev_place, levs, fields):
    waves, _, slots, count = twiddle.shape
    _, _, lats, modes, _ = blocks[0].shape
    rows = lats * modes * len(fields)
    width = NLON // levs + LANES
    depth = waves * PARTS * slots
    return pl.pallas_call(
        functools.partial(synthesis_kernel, waves, levs, fields),
        out_shape=[jax.ShapeDtypeStruct((rows, width), jnp.bfloat16)] * levs,
        in_specs=[pl.BlockSpec(memory_space=pltpu.SMEM)] * 2 + [vmem()] * (waves + 2),
        out_specs=[vmem()] * levs,
        scratch_shapes=[
            pltpu.VMEM((2 * rows, depth), jnp.bfloat16),
            pltpu.VMEM((levs, rows, width), jnp.bfloat16),
        ],
        compiler_params=pltpu.CompilerParams(vmem_limit_bytes=12 << 20),
        cost_estimate=cost(4 * rows * depth * count, 2 * depth * count),
        name="synthesis",
    )(wave_place, lev_place, *blocks, sign, twiddle)


def three_terms(matrix):
    high = matrix.astype(jnp.bfloat16)
    rest = matrix - high.astype(jnp.float32)
    middle = rest.astype(jnp.bfloat16)
    low = (rest - middle.astype(jnp.float32)).astype(jnp.bfloat16)
    return jnp.concatenate([high, middle, low], axis=0)


def levels_of(terms, place, blocks, gathered, base, modes):
    count = terms.shape[0] // 3
    for e, block in enumerate(blocks):
        start = pl.multiple_of((place ^ e) * modes, modes)
        gathered[pl.ds(start, modes)] = block[base : base + modes].astype(jnp.float32)
    rows = gathered[...].astype(jnp.bfloat16)
    result = jnp.dot(terms, rows, preferred_element_type=jnp.float32)
    return result[:count] + (result[count : 2 * count] + result[2 * count :])


def keep_edges(lat, lats, values, odd, pair_ref, diagonal_ref):
    edge = values.astype(jnp.bfloat16)
    if 0 < lat < lats - 1:
        return
    takes_pair = 1 if lat == 0 else 0

    @pl.when(odd == takes_pair)
    def _():
        pair_ref[...] = edge

    @pl.when(odd != takes_pair)
    def _():
        diagonal_ref[...] = edge


def tracer_kernel(modes, odd_ref, lev_ref, vertical_ref, *refs):
    blocks, (field_ref, pair_ref, diagonal_ref, gathered) = refs[:-4], refs[-4:]
    terms = three_terms(vertical_ref[...])
    lats = field_ref.shape[0]
    for lat in range(lats):
        values = levels_of(terms, lev_ref[0], blocks, gathered, lat * modes, modes)
        field_ref[lat] = values
        keep_edges(lat, lats, values, odd_ref[0], pair_ref, diagonal_ref)


def upwind(center, western, eastern, northern, southern, courant_x, courant_y):
    return (
        center
        - jnp.maximum(courant_x, 0.0) * (center - western)
        - jnp.minimum(courant_x, 0.0) * (eastern - center)
        - jnp.maximum(courant_y, 0.0) * (center - northern)
        - jnp.minimum(courant_y, 0.0) * (southern - center)
    )


def stepped(lat, odd_ref, end_ref, tracer_ref, pair_ref, diagonal_ref, courant_x, courant_y):
    lats, _, width = tracer_ref.shape
    center = tracer_ref[lat]

    def outside(takes_pair):
        pair = pair_ref[...].astype(jnp.float32)
        diagonal = jnp.where(end_ref[0] == 1, 0.0, diagonal_ref[...].astype(jnp.float32))
        return jnp.where(odd_ref[0] == takes_pair, pair, diagonal)

    northern = tracer_ref[lat - 1] if lat > 0 else outside(1)
    southern = tracer_ref[lat + 1] if lat < lats - 1 else outside(0)
    return upwind(
        center,
        pltpu.roll(center, 1, 1),
        pltpu.roll(center, width - 1, 1),
        northern,
        southern,
        courant_x,
        courant_y,
    )


def first_step_kernel(
    modes, odd_ref, end_ref, lev_ref, vertical_ref, tracer_ref, pair_ref, diagonal_ref, *refs
):
    blocks, (x_ref, y_ref, out_ref, next_pair_ref, next_diagonal_ref, gathered) = refs[:-6], refs[-6:]
    terms = three_terms(vertical_ref[...])
    lats = tracer_ref.shape[0]

    def courant(field, lat):
        base = (field * lats + lat) * modes
        velocity = levels_of(terms, lev_ref[0], blocks, gathered.at[field], base, modes)
        return courant_max * jnp.tanh(velocity)

    for lat in (0, lats - 1, *range(1, lats - 1)):
        courant_x, courant_y = courant(0, lat), courant(1, lat)
        x_ref[lat] = courant_x
        y_ref[lat] = courant_y
        values = stepped(
            lat, odd_ref, end_ref, tracer_ref, pair_ref, diagonal_ref, courant_x, courant_y
        )
        out_ref[lat] = values
        keep_edges(lat, lats, values, odd_ref[0], next_pair_ref, next_diagonal_ref)


def second_step_kernel(odd_ref, end_ref, tracer_ref, pair_ref, diagonal_ref, x_ref, y_ref, out_ref):
    width = out_ref.shape[2]
    for lat in range(tracer_ref.shape[0]):
        values = stepped(
            lat, odd_ref, end_ref, tracer_ref, pair_ref, diagonal_ref, x_ref[lat], y_ref[lat]
        )
        out_ref[:, lat, :] = values[:, :width]


def local_call(kernel, outs, scratch, *operands):
    smem = pl.BlockSpec(memory_space=pltpu.SMEM)
    return pl.pallas_call(
        kernel,
        out_shape=outs,
        in_specs=[smem if operand.dtype == jnp.int32 else vmem() for operand in operands],
        out_specs=jax.tree.map(lambda _: vmem(), outs),
        scratch_shapes=scratch,
        compiler_params=pltpu.CompilerParams(vmem_limit_bytes=16 << 20),
        cost_estimate=cost(4_000_000, 4_000_000),
    )(*operands)


def exchange(blocks, axis):
    count = lax.axis_size(axis)
    moved = [blocks[0]]
    for d in range(1, count):
        moved.append(lax.ppermute(blocks[d], axis, [(i, i ^ d) for i in range(count)]))
    return moved


def edges(pair, diagonal):
    count = lax.axis_size("wave")
    steps = [(i, i + 1) for i in range(1, count - 1, 2)] + [(0, 0)]
    steps = steps + [(b, a) for a, b in steps[:-1]] + [(count - 1, count - 1)]
    diagonal = lax.ppermute(diagonal, "wave", steps)
    pair = lax.ppermute(pair, "wave", [(i, i ^ 1) for i in range(count)])
    return pair, diagonal


def tiled_body(spectrum, legendre, wave_numbers, vertical):
    waves, levs = lax.axis_size("wave"), lax.axis_size("lev")
    slots, _, modes, _ = spectrum.shape
    levels = vertical.shape[0]
    lats = 2 * legendre.shape[2] // waves
    width = NLON // levs
    wave_place, lev_place = lax.axis_index("wave"), lax.axis_index("lev")
    at_end = (wave_place == 0) | (wave_place == waves - 1)
    odd, at_end = lax.rem(wave_place, 2)[None], at_end.astype(jnp.int32)[None]
    wave_place, lev_place = wave_place[None], lev_place[None]

    fourier = legendre_stage(spectrum, legendre, wave_numbers, wave_place, waves)
    by_wave = wave_numbers.reshape(waves, slots)
    sign = jnp.where(by_wave % 2 == 0, 1.0, -1.0).astype(jnp.bfloat16)[:, None, :]
    twiddle = twiddle_stage(by_wave, wave_place)
    received = exchange(fourier, "wave")
    columns = [
        exchange(
            synthesis_stage(received, sign, twiddle, wave_place, lev_place, levs, fields), "lev"
        )
        for fields in ((2,), (0, 1))
    ]

    whole = jax.ShapeDtypeStruct((lats, levels, width + LANES), jnp.float32)
    row = jax.ShapeDtypeStruct((levels, width + LANES), jnp.bfloat16)
    gathered = (levs * modes, width + LANES)
    tracer, pair, diagonal = local_call(
        functools.partial(tracer_kernel, modes),
        (whole, row, row),
        [pltpu.VMEM(gathered, jnp.float32)],
        odd,
        lev_place,
        vertical,
        *columns[0],
    )
    pair, diagonal = edges(pair, diagonal)
    courant_x, courant_y, tracer, next_pair, next_diagonal = local_call(
        functools.partial(first_step_kernel, modes),
        (whole, whole, whole, row, row),
        [pltpu.VMEM((2, *gathered), jnp.float32)],
        odd,
        at_end,
        lev_place,
        vertical,
        tracer,
        pair,
        diagonal,
        *columns[1],
    )
    pair, diagonal = edges(next_pair, next_diagonal)
    return local_call(
        second_step_kernel,
        jax.ShapeDtypeStruct((levels, lats, width), jnp.float32),
        [],
        odd,
        at_end,
        tracer,
        pair,
        diagonal,
        courant_x,
        courant_y,
    )


def body(spectrum, legendre, wave_numbers, vertical):
    waves, levs = lax.axis_size("wave"), lax.axis_size("lev")
    slots, degrees, modes, _ = spectrum.shape
    tiled = (
        slots % LANES == 0
        and slots % (2 * PAIRS) == 0
        and slots > 2 * PAIRS * AHEAD
        and legendre.shape[2] % 16 == 0
        and modes % 8 == 0
        and degrees % CHUNK == 0
        and waves & (waves - 1) == 0
        and levs & (levs - 1) == 0
        and NLON // levs % TILE == 0
        and levs % 2 == 0
        and 2 * legendre.shape[2] // waves >= 2
    )
    form = tiled_body if tiled else plain_body
    return form(spectrum, legendre, wave_numbers, vertical)


def solution(mesh):
    in_specs = (P("wave", None, "lev", None), P("wave", None, None), P(), P())
    out_specs = P(None, "wave", "lev")
    return jax.shard_map(body, mesh=mesh, in_specs=in_specs, out_specs=out_specs, check_vma=False)
```

```python
import functools
import math

import jax
import jax.numpy as jnp
from jax import lax
from jax.experimental import pallas as pl
from jax.experimental.pallas import tpu as pltpu
from jax.sharding import PartitionSpec as P

NLON = 2048
FIELDS = 3
PARTS = 2
LANES = 128
CHUNK = 256
TILE = 256
PAIRS = 8
GROUP = 4
AHEAD = 7

courant_max = 0.45


def padded(block, sides, width, periodic):
    for axis, dim in sides:
        count = lax.axis_size(axis)
        forward = [(i, i + 1) for i in range(count - 1)]
        if periodic:
            forward.append((count - 1, 0))
        backward = [(target, source) for source, target in forward]
        low = lax.ppermute(
            lax.slice_in_dim(block, block.shape[dim] - width, None, axis=dim), axis, forward
        )
        high = lax.ppermute(lax.slice_in_dim(block, 0, width, axis=dim), axis, backward)
        block = jnp.concatenate([low, block, high], axis=dim)
    return block


def twiddles(numbers):
    longitude = jnp.arange(NLON, dtype=jnp.int32)
    residue = numbers[:, None] * longitude[None, :] % NLON
    angles = residue.astype(jnp.float32) * (2.0 * math.pi / NLON)
    weight = jnp.where(numbers == 0, 1.0, 2.0).astype(jnp.float32)[:, None]
    return jnp.stack([weight * jnp.cos(angles), -weight * jnp.sin(angles)]).astype(jnp.bfloat16)


def parity_columns(coefficient, degree, lengths):
    counted = degree < lengths[:, None]
    even_mask = counted & (degree % 2 == 0)
    odd_mask = counted & (degree % 2 == 1)
    return jnp.concatenate(
        [
            jnp.where(even_mask[:, :, None], coefficient, 0),
            jnp.where(odd_mask[:, :, None], coefficient, 0),
        ],
        axis=2,
    )


def padded_sums(coefficient, basis, own_numbers):
    degree_count = coefficient.shape[1]
    degree = jnp.arange(degree_count, dtype=jnp.int32)[None, :]
    masked = parity_columns(coefficient, degree, degree_count - own_numbers)
    return jnp.einsum("skc,ski->sci", masked, basis, preferred_element_type=jnp.float32)


def upwind_core(extended, courant_x, courant_y):
    center = extended[:, 1:-1, 1:-1]
    western = extended[:, 1:-1, :-2]
    eastern = extended[:, 1:-1, 2:]
    northern = extended[:, :-2, 1:-1]
    southern = extended[:, 2:, 1:-1]
    return (
        center
        - jnp.maximum(courant_x, 0.0) * (center - western)
        - jnp.minimum(courant_x, 0.0) * (eastern - center)
        - jnp.maximum(courant_y, 0.0) * (center - northern)
        - jnp.minimum(courant_y, 0.0) * (southern - center)
    )


def plain_body(spectrum, legendre, wave_numbers, vertical):
    slot_count, degree_count, level_count, part_count = spectrum.shape
    columns = level_count * part_count
    coefficient = spectrum.reshape(slot_count, degree_count, columns)
    first_slot = lax.axis_index("wave") * slot_count
    own_numbers = lax.dynamic_slice_in_dim(wave_numbers, first_slot, slot_count)
    partial_sums = padded_sums(coefficient, legendre, own_numbers)
    even_sums = partial_sums[:, :columns]
    odd_sums = partial_sums[:, columns:]
    northern = even_sums + odd_sums
    southern = jnp.flip(even_sums - odd_sums, axis=2)
    fourier = jnp.concatenate([northern, southern], axis=2).astype(jnp.bfloat16)
    received = lax.all_to_all(fourier, "wave", split_axis=2, concat_axis=0, tiled=True)
    lat_count = received.shape[2]
    received = received.reshape(received.shape[0], level_count, FIELDS, PARTS, lat_count)
    twiddle = twiddles(wave_numbers)
    grid_values = jnp.einsum(
        "smfrl,rsj->lmfj", received, twiddle, preferred_element_type=jnp.float32
    ).astype(jnp.bfloat16)
    column_values = lax.all_to_all(grid_values, "lev", split_axis=3, concat_axis=1, tiled=True)
    fields = jnp.einsum(
        "vm,lmfj->fvlj",
        vertical,
        column_values.astype(jnp.float32),
        precision=lax.Precision.HIGHEST,
    )
    courant_x = courant_max * jnp.tanh(fields[0])
    courant_y = courant_max * jnp.tanh(fields[1])
    tracer = fields[2]
    for _ in range(2):
        extended = padded(tracer, (("wave", 1),), 1, False)
        extended = padded(extended, (("lev", 2),), 1, True)
        tracer = upwind_core(extended, courant_x, courant_y)
    return tracer


def vmem():
    return pl.BlockSpec(memory_space=pltpu.VMEM)


def cost(flops, count_bytes):
    return pl.CostEstimate(flops=flops, bytes_accessed=count_bytes, transcendentals=0)


def legendre_kernel(numbers_ref, place_ref, spectrum_ref, legendre_ref, *refs):
    outs, (held, basis_held, order, sums, arrived) = refs[:-5], refs[-5:]
    waves = len(outs)
    _, _, lats, modes, _ = outs[0].shape
    buffers, pairs, rows, _ = held.shape
    slots, half, degrees = legendre_ref.shape
    chunks = degrees // CHUNK + 1
    steps = slots // (2 * pairs)
    ahead = buffers - 1
    place = place_ref[0]
    many = 2 * GROUP

    def plan(index):
        first = degrees - numbers_ref[place * slots + 2 * index]
        second = degrees - numbers_ref[place * slots + 2 * index + 1]
        return first, second, lax.shift_right_logical(first + (CHUNK - 1), CHUNK.bit_length() - 1)

    def fetch(group, slot):
        pltpu.make_async_copy(
            legendre_ref.at[pl.ds(group * 2 * pairs, 2 * pairs)],
            basis_held.at[slot],
            arrived.at[slot],
        ).start()
        for pair in range(pairs):
            index = group * pairs + pair
            _, _, edge = plan(index)
            for t in range(chunks):
                inside = t < edge
                source = jnp.where(inside, 2 * index, 2 * index + 1)
                block = jnp.where(inside, t, t - edge)
                start = pl.multiple_of(block * CHUNK, CHUNK)
                pltpu.make_async_copy(
                    spectrum_ref.at[source, :, pl.ds(start, CHUNK)],
                    held.at[slot, pair, :, pl.ds(t * CHUNK, CHUNK)],
                    arrived.at[slot],
                ).start()

    for group in range(min(ahead, steps)):
        fetch(group, group)

    row = lax.broadcasted_iota(jnp.int32, order.shape, 0)
    column = lax.broadcasted_iota(jnp.int32, order.shape, 1)
    wanted = lax.rem(row, many) * (2 * half) + lax.div(row, many)
    order[...] = jnp.where(column == wanted, 1.0, 0.0).astype(jnp.bfloat16)

    def work(step, fetches):
        now = lax.rem(step, buffers)
        for buffer in (held, basis_held):
            pltpu.make_async_copy(buffer.at[now], buffer.at[now], arrived.at[now]).wait()
        if fetches:
            fetch(step + ahead, lax.rem(step + ahead, buffers))
        lane = lax.broadcasted_iota(jnp.int32, (half, CHUNK), 1)
        sign = jnp.where(lane % 2 == 0, 1.0, -1.0).astype(jnp.bfloat16)
        for pair in range(pairs):
            index = step * pairs + pair
            first, second, edge = plan(index)
            columns = []
            for t in range(chunks):
                inside = t < edge
                local = jnp.where(inside, 2 * pair, 2 * pair + 1)
                block = jnp.where(inside, t, t - edge)
                start = pl.multiple_of(block * CHUNK, CHUNK)
                length = jnp.where(inside, first, second) - start
                values = basis_held[now, local, :, pl.ds(start, CHUNK)]
                own = jnp.where(inside, length, 0)
                own_mask = jnp.where(lane < own, 1.0, 0.0).astype(jnp.bfloat16)
                other_mask = jnp.where(lane < length - own, 1.0, 0.0).astype(jnp.bfloat16)
                flip = values * sign
                columns.append(
                    jnp.concatenate([values * own_mask, flip * own_mask, values * other_mask, flip * other_mask], axis=0)
                )
            result = lax.dot_general(
                jnp.concatenate(columns, axis=1),
                held[now, pair],
                (((1,), (1,)), ((), ())),
                preferred_element_type=jnp.float32,
            )
            for which in range(2):
                part = result[which * 2 * half : (which + 1) * 2 * half]
                for low in range(0, rows, LANES):
                    width = min(LANES, rows - low)
                    sums[low // LANES, pl.ds(2 * index + which, 2 * half, stride=slots), :width] = (
                        part[:, low : low + width]
                    )

    lax.fori_loop(0, steps - ahead, lambda step, _: work(step, True), None)
    lax.fori_loop(steps - ahead, steps, lambda step, _: work(step, False), None)

    for d in range(waves):
        for l in range(lats):
            lat = (place ^ d) * lats + l
            row = jnp.where(lat < half, lat, 3 * half - 1 - lat)
            turned = [
                sums[low // LANES, pl.ds(pl.multiple_of(row * slots, slots), slots), :].T.astype(jnp.bfloat16) for low in range(0, rows, LANES)
            ]
            whole = jnp.concatenate(turned, axis=0)
            for f in range(FIELDS):
                for p in range(PARTS):
                    base = (f * PARTS + p) * modes
                    outs[d][f, p, l] = whole[base : base + modes]


def legendre_stage(spectrum, legendre, numbers, place, waves):
    slots, degrees, modes, _ = spectrum.shape
    half = legendre.shape[2]
    lats = 2 * half // waves
    rows = modes * FIELDS * PARTS
    turned = jnp.transpose(spectrum, (0, 3, 2, 1)).reshape(slots, rows, degrees)
    basis = jnp.transpose(legendre, (0, 2, 1))
    chunks = degrees // CHUNK + 1
    tiles = -(-rows // LANES)
    smem = pl.BlockSpec(memory_space=pltpu.SMEM)
    away = pl.BlockSpec(memory_space=pl.ANY)
    return pl.pallas_call(
        legendre_kernel,
        out_shape=[jax.ShapeDtypeStruct((FIELDS, PARTS, lats, modes, slots), jnp.bfloat16)] * waves,
        in_specs=[smem, smem, away, away],
        out_specs=[vmem()] * waves,
        scratch_shapes=[
            pltpu.VMEM((AHEAD + 1, PAIRS, rows, chunks * CHUNK), jnp.bfloat16),
            pltpu.VMEM((AHEAD + 1, 2 * PAIRS, half, degrees), jnp.bfloat16),
            pltpu.VMEM((GROUP * 4 * half, GROUP * 4 * half), jnp.bfloat16),
            pltpu.VMEM((tiles, 2 * half * slots, LANES), jnp.float32),
            pltpu.SemaphoreType.DMA((AHEAD + 1,)),
        ],
        compiler_params=pltpu.CompilerParams(vmem_limit_bytes=58 << 20),
        cost_estimate=cost(slots * rows * degrees * 2 * half, slots * rows * degrees),
        name="legendre_sums",
    )(numbers, place, turned, basis)


def twiddle_kernel(place_ref, low_cos_ref, low_sin_ref, turn_cos_ref, turn_sin_ref, out_ref):
    slots = low_cos_ref.shape[1]
    shape = (LANES, slots)
    turn_cos = jnp.broadcast_to(turn_cos_ref[0], shape).T
    turn_sin = jnp.broadcast_to(turn_sin_ref[0], shape).T
    cos, sin = low_cos_ref[0], low_sin_ref[0]
    for block in range(out_ref.shape[3] // LANES):
        lanes = pl.ds(block * LANES, LANES)
        out_ref[0, 0, :, lanes] = cos.astype(jnp.bfloat16)
        out_ref[0, 1, :, lanes] = (-sin).astype(jnp.bfloat16)
        cos, sin = cos * turn_cos - sin * turn_sin, sin * turn_cos + cos * turn_sin


def twiddle_stage(numbers, place):
    waves, slots = numbers.shape
    count = NLON // 2

    def angles(residue):
        return (residue % NLON).astype(jnp.float32) * (2.0 * math.pi / NLON)

    low = angles(numbers[:, :, None] * jnp.arange(LANES, dtype=jnp.int32)[None, None, :])
    turn = angles(numbers * LANES)[:, None, :]
    weight = jnp.where(numbers == 0, 1.0, 2.0).astype(jnp.float32)[:, :, None]

    def spec(rows, last):
        return pl.BlockSpec((1, rows, last), lambda i, place_ref: (place_ref[0] ^ i, 0, 0))

    return pl.pallas_call(
        twiddle_kernel,
        out_shape=jax.ShapeDtypeStruct((waves, PARTS, slots, count), jnp.bfloat16),
        grid_spec=pltpu.PrefetchScalarGridSpec(
            num_scalar_prefetch=1,
            grid=(waves,),
            in_specs=[spec(slots, LANES), spec(slots, LANES), spec(1, slots), spec(1, slots)],
            out_specs=pl.BlockSpec((1, PARTS, slots, count), lambda i, _: (i, 0, 0, 0)),
        ),
        compiler_params=pltpu.CompilerParams(vmem_limit_bytes=8 << 20),
        cost_estimate=cost(8 * waves * slots * count, 4 * waves * slots * count),
        name="twiddles",
    )(place, weight * jnp.cos(low), weight * jnp.sin(low), jnp.cos(turn), jnp.sin(turn))


def synthesis_kernel(waves, levs, fields, wave_ref, lev_ref, *refs):
    blocks, (sign_ref, twiddle_ref) = refs[:waves], refs[waves : waves + 2]
    outs, (left, grid) = refs[waves + 2 : -2], refs[-2:]
    _, _, lats, modes, slots = blocks[0].shape
    each = lats * modes
    rows = each * len(fields)
    for d in range(waves):
        sign = sign_ref[wave_ref[0] ^ d]
        for p in range(PARTS):
            lanes = pl.ds((d * PARTS + p) * slots, slots)
            for place, field in enumerate(fields):
                values = blocks[d][field, p].reshape(each, slots)
                left[place * each : (place + 1) * each, lanes] = values
                left[rows + place * each : rows + (place + 1) * each, lanes] = values * sign

    width = NLON // levs
    ratio = width // TILE
    steps = twiddle_ref.shape[3] // TILE
    lane = lax.broadcasted_iota(jnp.int32, (rows, LANES), 1)
    for step in range(steps):
        right = twiddle_ref[:, :, :, pl.ds(step * TILE, TILE)]
        right = right.reshape(waves * PARTS * slots, TILE)
        result = jnp.dot(left[...], right, preferred_element_type=jnp.float32)
        result = result.astype(jnp.bfloat16)
        for which in range(2):
            owner, inner = divmod(step + which * steps, ratio)
            grid[owner, :, pl.ds(inner * TILE, TILE)] = result[which * rows : (which + 1) * rows]
    for owner in range(levs):
        grid[owner, :, pl.ds(width, LANES)] = jnp.where(
            lane < LANES // 2,
            grid[(owner + 1) % levs, :, :LANES],
            grid[(owner - 1) % levs, :, pl.ds(width - LANES, LANES)],
        )
    place = lev_ref[0]
    for e in range(levs):
        outs[e][...] = grid[place ^ e]


def synthesis_stage(blocks, sign, twiddle, wave_place, lev_place, levs, fields):
    waves, _, slots, count = twiddle.shape
    _, _, lats, modes, _ = blocks[0].shape
    rows = lats * modes * len(fields)
    width = NLON // levs + LANES
    depth = waves * PARTS * slots
    return pl.pallas_call(
        functools.partial(synthesis_kernel, waves, levs, fields),
        out_shape=[jax.ShapeDtypeStruct((rows, width), jnp.bfloat16)] * levs,
        in_specs=[pl.BlockSpec(memory_space=pltpu.SMEM)] * 2 + [vmem()] * (waves + 2),
        out_specs=[vmem()] * levs,
        scratch_shapes=[
            pltpu.VMEM((2 * rows, depth), jnp.bfloat16),
            pltpu.VMEM((levs, rows, width), jnp.bfloat16),
        ],
        compiler_params=pltpu.CompilerParams(vmem_limit_bytes=12 << 20),
        cost_estimate=cost(4 * rows * depth * count, 2 * depth * count),
        name="synthesis",
    )(wave_place, lev_place, *blocks, sign, twiddle)


def three_terms(matrix):
    high = matrix.astype(jnp.bfloat16)
    rest = matrix - high.astype(jnp.float32)
    middle = rest.astype(jnp.bfloat16)
    low = (rest - middle.astype(jnp.float32)).astype(jnp.bfloat16)
    return jnp.concatenate([high, middle, low], axis=0)


def levels_of(terms, place, blocks, gathered, base, modes):
    count = terms.shape[0] // 3
    for e, block in enumerate(blocks):
        start = pl.multiple_of((place ^ e) * modes, modes)
        gathered[pl.ds(start, modes)] = block[base : base + modes].astype(jnp.float32)
    rows = gathered[...].astype(jnp.bfloat16)
    result = jnp.dot(terms, rows, preferred_element_type=jnp.float32)
    return result[:count] + (result[count : 2 * count] + result[2 * count :])


def keep_edges(lat, lats, values, odd, pair_ref, diagonal_ref):
    edge = values.astype(jnp.bfloat16)
    if 0 < lat < lats - 1:
        return
    takes_pair = 1 if lat == 0 else 0

    @pl.when(odd == takes_pair)
    def _():
        pair_ref[...] = edge

    @pl.when(odd != takes_pair)
    def _():
        diagonal_ref[...] = edge


def tracer_kernel(modes, odd_ref, lev_ref, vertical_ref, *refs):
    blocks, (field_ref, pair_ref, diagonal_ref, gathered) = refs[:-4], refs[-4:]
    terms = three_terms(vertical_ref[...])
    lats = field_ref.shape[0]
    for lat in range(lats):
        values = levels_of(terms, lev_ref[0], blocks, gathered, lat * modes, modes)
        field_ref[lat] = values
        keep_edges(lat, lats, values, odd_ref[0], pair_ref, diagonal_ref)


def upwind(center, western, eastern, northern, southern, courant_x, courant_y):
    return (
        center
        - jnp.maximum(courant_x, 0.0) * (center - western)
        - jnp.minimum(courant_x, 0.0) * (eastern - center)
        - jnp.maximum(courant_y, 0.0) * (center - northern)
        - jnp.minimum(courant_y, 0.0) * (southern - center)
    )


def row_step(center, northern, southern, courant_x, courant_y):
    width = center.shape[1]
    western, eastern = pltpu.roll(center, 1, 1), pltpu.roll(center, width - 1, 1)
    return upwind(center, western, eastern, northern, southern, courant_x, courant_y)


def outside(takes_pair, odd_ref, end_ref, pair_ref, diagonal_ref):
    pair = pair_ref[...].astype(jnp.float32)
    diagonal = jnp.where(end_ref[0] == 1, 0.0, diagonal_ref[...].astype(jnp.float32))
    return jnp.where(odd_ref[0] == takes_pair, pair, diagonal)


def courants(lev_ref, vertical_ref, blocks, gathered, lats, modes):
    terms = three_terms(vertical_ref[...])

    def of(field, lat):
        base = (field * lats + lat) * modes
        velocity = levels_of(terms, lev_ref[0], blocks, gathered.at[field], base, modes)
        return courant_max * jnp.tanh(velocity)

    return of


def edge_step_kernel(
    modes, odd_ref, end_ref, lev_ref, vertical_ref, tracer_ref, pair_ref, diagonal_ref, *refs
):
    blocks, (x_ref, y_ref, out_ref, next_pair_ref, next_diagonal_ref, gathered) = refs[:-6], refs[-6:]
    lats = tracer_ref.shape[0]
    courant = courants(lev_ref, vertical_ref, blocks, gathered, lats, modes)
    for place, lat in enumerate((0, lats - 1)):
        other = outside(1 - place, odd_ref, end_ref, pair_ref, diagonal_ref)
        northern = other if place == 0 else tracer_ref[lat - 1]
        southern = tracer_ref[lat + 1] if place == 0 else other
        x_ref[place], y_ref[place] = courant(0, lat), courant(1, lat)
        values = row_step(tracer_ref[lat], northern, southern, x_ref[place], y_ref[place])
        out_ref[place] = values
        keep_edges(lat, lats, values, odd_ref[0], next_pair_ref, next_diagonal_ref)


def inner_steps_kernel(modes, lev_ref, vertical_ref, tracer_ref, edge_ref, *refs):
    blocks, (inner_ref, out_ref, x_ref, y_ref, gathered) = refs[:-5], refs[-5:]
    lats = tracer_ref.shape[0]
    width = out_ref.shape[2]
    courant = courants(lev_ref, vertical_ref, blocks, gathered, lats, modes)
    inner = lats - 2
    for place in range(inner):
        lat = place + 1
        x_ref[place], y_ref[place] = courant(0, lat), courant(1, lat)
        inner_ref[place] = row_step(
            tracer_ref[lat], tracer_ref[lat - 1], tracer_ref[lat + 1], x_ref[place], y_ref[place]
        )
    for place in range(inner):
        northern = inner_ref[place - 1] if place > 0 else edge_ref[0]
        southern = inner_ref[place + 1] if place < inner - 1 else edge_ref[1]
        values = row_step(inner_ref[place], northern, southern, x_ref[place], y_ref[place])
        out_ref[place] = values[:, :width]


def last_step_kernel(
    odd_ref, end_ref, edge_ref, inner_ref, done_ref, pair_ref, diagonal_ref, x_ref, y_ref, out_ref
):
    inner, _, width = done_ref.shape
    for place in range(inner):
        out_ref[:, place + 1, :] = done_ref[place]
    for place in range(2):
        other = outside(1 - place, odd_ref, end_ref, pair_ref, diagonal_ref)
        northern = other if place == 0 else inner_ref[inner - 1]
        southern = inner_ref[0] if place == 0 else other
        values = row_step(edge_ref[place], northern, southern, x_ref[place], y_ref[place])
        out_ref[:, place * (inner + 1), :] = values[:, :width]


def local_call(kernel, outs, scratch, *operands):
    smem = pl.BlockSpec(memory_space=pltpu.SMEM)
    return pl.pallas_call(
        kernel,
        out_shape=outs,
        in_specs=[smem if operand.dtype == jnp.int32 else vmem() for operand in operands],
        out_specs=jax.tree.map(lambda _: vmem(), outs),
        scratch_shapes=scratch,
        compiler_params=pltpu.CompilerParams(vmem_limit_bytes=16 << 20),
        cost_estimate=cost(4_000_000, 4_000_000),
    )(*operands)


def exchange(blocks, axis):
    count = lax.axis_size(axis)
    moved = [blocks[0]]
    for d in range(1, count):
        moved.append(lax.ppermute(blocks[d], axis, [(i, i ^ d) for i in range(count)]))
    return moved


def edges(pair, diagonal):
    count = lax.axis_size("wave")
    steps = [(i, i + 1) for i in range(1, count - 1, 2)] + [(0, 0)]
    steps = steps + [(b, a) for a, b in steps[:-1]] + [(count - 1, count - 1)]
    diagonal = lax.ppermute(diagonal, "wave", steps)
    pair = lax.ppermute(pair, "wave", [(i, i ^ 1) for i in range(count)])
    return pair, diagonal


def tiled_body(spectrum, legendre, wave_numbers, vertical):
    waves, levs = lax.axis_size("wave"), lax.axis_size("lev")
    slots, _, modes, _ = spectrum.shape
    levels = vertical.shape[0]
    lats = 2 * legendre.shape[2] // waves
    width = NLON // levs
    wave_place, lev_place = lax.axis_index("wave"), lax.axis_index("lev")
    at_end = (wave_place == 0) | (wave_place == waves - 1)
    odd, at_end = lax.rem(wave_place, 2)[None], at_end.astype(jnp.int32)[None]
    wave_place, lev_place = wave_place[None], lev_place[None]

    fourier = legendre_stage(spectrum, legendre, wave_numbers, wave_place, waves)
    by_wave = wave_numbers.reshape(waves, slots)
    sign = jnp.where(by_wave % 2 == 0, 1.0, -1.0).astype(jnp.bfloat16)[:, None, :]
    twiddle = twiddle_stage(by_wave, wave_place)
    received = exchange(fourier, "wave")
    columns = [
        exchange(
            synthesis_stage(received, sign, twiddle, wave_place, lev_place, levs, fields), "lev"
        )
        for fields in ((2,), (0, 1))
    ]

    whole = jax.ShapeDtypeStruct((lats, levels, width + LANES), jnp.float32)
    row = jax.ShapeDtypeStruct((levels, width + LANES), jnp.bfloat16)
    pair_of_rows = jax.ShapeDtypeStruct((2, *whole.shape[1:]), jnp.float32)
    gathered = (levs * modes, width + LANES)
    tracer, pair, diagonal = local_call(
        functools.partial(tracer_kernel, modes),
        (whole, row, row),
        [pltpu.VMEM(gathered, jnp.float32)],
        odd,
        lev_place,
        vertical,
        *columns[0],
    )
    pair, diagonal = edges(pair, diagonal)
    courant_x, courant_y, edge, pair, diagonal = local_call(
        functools.partial(edge_step_kernel, modes),
        (pair_of_rows, pair_of_rows, pair_of_rows, row, row),
        [pltpu.VMEM((2, *gathered), jnp.float32)],
        odd,
        at_end,
        lev_place,
        vertical,
        tracer,
        pair,
        diagonal,
        *columns[1],
    )
    pair, diagonal = edges(pair, diagonal)
    inner, done = local_call(
        functools.partial(inner_steps_kernel, modes),
        (
            jax.ShapeDtypeStruct((lats - 2, levels, width + LANES), jnp.float32),
            jax.ShapeDtypeStruct((lats - 2, levels, width), jnp.float32),
        ),
        [
            pltpu.VMEM((lats - 2, levels, width + LANES), jnp.float32),
            pltpu.VMEM((lats - 2, levels, width + LANES), jnp.float32),
            pltpu.VMEM((2, *gathered), jnp.float32),
        ],
        lev_place,
        vertical,
        tracer,
        edge,
        *columns[1],
    )
    return local_call(
        last_step_kernel,
        jax.ShapeDtypeStruct((levels, lats, width), jnp.float32),
        [],
        odd,
        at_end,
        edge,
        inner,
        done,
        pair,
        diagonal,
        courant_x,
        courant_y,
    )


def body(spectrum, legendre, wave_numbers, vertical):
    waves, levs = lax.axis_size("wave"), lax.axis_size("lev")
    slots, degrees, modes, _ = spectrum.shape
    tiled = (
        slots % LANES == 0
        and slots % (2 * PAIRS) == 0
        and slots > 2 * PAIRS * AHEAD
        and legendre.shape[2] % 16 == 0
        and modes % 8 == 0
        and degrees % CHUNK == 0
        and waves & (waves - 1) == 0
        and levs & (levs - 1) == 0
        and NLON // levs % TILE == 0
        and levs % 2 == 0
        and 2 * legendre.shape[2] // waves >= 3
    )
    form = tiled_body if tiled else plain_body
    return form(spectrum, legendre, wave_numbers, vertical)


def solution(mesh):
    in_specs = (P("wave", None, "lev", None), P("wave", None, None), P(), P())
    out_specs = P(None, "wave", "lev")
    return jax.shard_map(body, mesh=mesh, in_specs=in_specs, out_specs=out_specs, check_vma=False)
```

```python
import functools
import math

import jax
import jax.numpy as jnp
from jax import lax
from jax.experimental import pallas as pl
from jax.experimental.pallas import tpu as pltpu
from jax.sharding import PartitionSpec as P

NLON = 2048
FIELDS = 3
PARTS = 2
LANES = 128
CHUNK = 256
TILE = 256
PAIRS = 8
HALO = 4
AHEAD = 7

courant_max = 0.45


def padded(block, sides, width, periodic):
    for axis, dim in sides:
        count = lax.axis_size(axis)
        forward = [(i, i + 1) for i in range(count - 1)]
        if periodic:
            forward.append((count - 1, 0))
        backward = [(target, source) for source, target in forward]
        low = lax.ppermute(
            lax.slice_in_dim(block, block.shape[dim] - width, None, axis=dim), axis, forward
        )
        high = lax.ppermute(lax.slice_in_dim(block, 0, width, axis=dim), axis, backward)
        block = jnp.concatenate([low, block, high], axis=dim)
    return block


def twiddles(numbers):
    longitude = jnp.arange(NLON, dtype=jnp.int32)
    residue = numbers[:, None] * longitude[None, :] % NLON
    angles = residue.astype(jnp.float32) * (2.0 * math.pi / NLON)
    weight = jnp.where(numbers == 0, 1.0, 2.0).astype(jnp.float32)[:, None]
    return jnp.stack([weight * jnp.cos(angles), -weight * jnp.sin(angles)]).astype(jnp.bfloat16)


def parity_columns(coefficient, degree, lengths):
    counted = degree < lengths[:, None]
    even_mask = counted & (degree % 2 == 0)
    odd_mask = counted & (degree % 2 == 1)
    return jnp.concatenate(
        [
            jnp.where(even_mask[:, :, None], coefficient, 0),
            jnp.where(odd_mask[:, :, None], coefficient, 0),
        ],
        axis=2,
    )


def padded_sums(coefficient, basis, own_numbers):
    degree_count = coefficient.shape[1]
    degree = jnp.arange(degree_count, dtype=jnp.int32)[None, :]
    masked = parity_columns(coefficient, degree, degree_count - own_numbers)
    return jnp.einsum("skc,ski->sci", masked, basis, preferred_element_type=jnp.float32)


def upwind_core(extended, courant_x, courant_y):
    center = extended[:, 1:-1, 1:-1]
    western = extended[:, 1:-1, :-2]
    eastern = extended[:, 1:-1, 2:]
    northern = extended[:, :-2, 1:-1]
    southern = extended[:, 2:, 1:-1]
    return (
        center
        - jnp.maximum(courant_x, 0.0) * (center - western)
        - jnp.minimum(courant_x, 0.0) * (eastern - center)
        - jnp.maximum(courant_y, 0.0) * (center - northern)
        - jnp.minimum(courant_y, 0.0) * (southern - center)
    )


def plain_body(spectrum, legendre, wave_numbers, vertical):
    slot_count, degree_count, level_count, part_count = spectrum.shape
    columns = level_count * part_count
    coefficient = spectrum.reshape(slot_count, degree_count, columns)
    first_slot = lax.axis_index("wave") * slot_count
    own_numbers = lax.dynamic_slice_in_dim(wave_numbers, first_slot, slot_count)
    partial_sums = padded_sums(coefficient, legendre, own_numbers)
    even_sums = partial_sums[:, :columns]
    odd_sums = partial_sums[:, columns:]
    northern = even_sums + odd_sums
    southern = jnp.flip(even_sums - odd_sums, axis=2)
    fourier = jnp.concatenate([northern, southern], axis=2).astype(jnp.bfloat16)
    received = lax.all_to_all(fourier, "wave", split_axis=2, concat_axis=0, tiled=True)
    lat_count = received.shape[2]
    received = received.reshape(received.shape[0], level_count, FIELDS, PARTS, lat_count)
    twiddle = twiddles(wave_numbers)
    grid_values = jnp.einsum(
        "smfrl,rsj->lmfj", received, twiddle, preferred_element_type=jnp.float32
    ).astype(jnp.bfloat16)
    column_values = lax.all_to_all(grid_values, "lev", split_axis=3, concat_axis=1, tiled=True)
    fields = jnp.einsum(
        "vm,lmfj->fvlj",
        vertical,
        column_values.astype(jnp.float32),
        precision=lax.Precision.HIGHEST,
    )
    courant_x = courant_max * jnp.tanh(fields[0])
    courant_y = courant_max * jnp.tanh(fields[1])
    tracer = fields[2]
    for _ in range(2):
        extended = padded(tracer, (("wave", 1),), 1, False)
        extended = padded(extended, (("lev", 2),), 1, True)
        tracer = upwind_core(extended, courant_x, courant_y)
    return tracer


def vmem():
    return pl.BlockSpec(memory_space=pltpu.VMEM)


def cost(flops, count_bytes):
    return pl.CostEstimate(flops=flops, bytes_accessed=count_bytes, transcendentals=0)


def legendre_kernel(numbers_ref, place_ref, spectrum_ref, legendre_ref, *refs):
    outs, (held, basis_held, sums, arrived) = refs[:-4], refs[-4:]
    waves = len(outs)
    _, _, lats, modes, _ = outs[0].shape
    buffers, pairs, rows, _ = held.shape
    slots, half, degrees = legendre_ref.shape
    chunks = degrees // CHUNK + 1
    steps = slots // (2 * pairs)
    ahead = buffers - 1
    place = place_ref[0]

    def plan(index):
        first = degrees - numbers_ref[place * slots + 2 * index]
        second = degrees - numbers_ref[place * slots + 2 * index + 1]
        return first, second, lax.shift_right_logical(first + (CHUNK - 1), CHUNK.bit_length() - 1)

    def fetch(group, slot):
        pltpu.make_async_copy(
            legendre_ref.at[pl.ds(group * 2 * pairs, 2 * pairs)],
            basis_held.at[slot],
            arrived.at[slot],
        ).start()
        for pair in range(pairs):
            index = group * pairs + pair
            _, _, edge = plan(index)
            for t in range(chunks):
                inside = t < edge
                source = jnp.where(inside, 2 * index, 2 * index + 1)
                block = jnp.where(inside, t, t - edge)
                start = pl.multiple_of(block * CHUNK, CHUNK)
                pltpu.make_async_copy(
                    spectrum_ref.at[source, :, pl.ds(start, CHUNK)],
                    held.at[slot, pair, :, pl.ds(t * CHUNK, CHUNK)],
                    arrived.at[slot],
                ).start()

    for group in range(min(ahead, steps)):
        fetch(group, group)

    def work(step, fetches):
        now = lax.rem(step, buffers)
        for buffer in (held, basis_held):
            pltpu.make_async_copy(buffer.at[now], buffer.at[now], arrived.at[now]).wait()
        if fetches:
            fetch(step + ahead, lax.rem(step + ahead, buffers))
        lane = lax.broadcasted_iota(jnp.int32, (half, CHUNK), 1)
        sign = jnp.where(lane % 2 == 0, 1.0, -1.0).astype(jnp.bfloat16)
        for pair in range(pairs):
            index = step * pairs + pair
            first, second, edge = plan(index)
            columns = []
            for t in range(chunks):
                inside = t < edge
                local = jnp.where(inside, 2 * pair, 2 * pair + 1)
                block = jnp.where(inside, t, t - edge)
                start = pl.multiple_of(block * CHUNK, CHUNK)
                length = jnp.where(inside, first, second) - start
                values = basis_held[now, local, :, pl.ds(start, CHUNK)]
                own = jnp.where(inside, length, 0)
                own_mask = jnp.where(lane < own, 1.0, 0.0).astype(jnp.bfloat16)
                other_mask = jnp.where(lane < length - own, 1.0, 0.0).astype(jnp.bfloat16)
                flip = values * sign
                columns.append(
                    jnp.concatenate([values * own_mask, flip * own_mask, values * other_mask, flip * other_mask], axis=0)
                )
            result = lax.dot_general(
                jnp.concatenate(columns, axis=1),
                held[now, pair],
                (((1,), (1,)), ((), ())),
                preferred_element_type=jnp.float32,
            )
            for which in range(2):
                part = result[which * 2 * half : (which + 1) * 2 * half]
                for low in range(0, rows, LANES):
                    width = min(LANES, rows - low)
                    sums[low // LANES, pl.ds(2 * index + which, 2 * half, stride=slots), :width] = (
                        part[:, low : low + width]
                    )

    lax.fori_loop(0, steps - ahead, lambda step, _: work(step, True), None)
    lax.fori_loop(steps - ahead, steps, lambda step, _: work(step, False), None)

    for d in range(waves):
        for l in range(lats):
            lat = (place ^ d) * lats + l
            row = jnp.where(lat < half, lat, 3 * half - 1 - lat)
            turned = [
                sums[low // LANES, pl.ds(pl.multiple_of(row * slots, slots), slots), :].T.astype(jnp.bfloat16) for low in range(0, rows, LANES)
            ]
            whole = jnp.concatenate(turned, axis=0)
            for f in range(FIELDS):
                for p in range(PARTS):
                    base = (f * PARTS + p) * modes
                    outs[d][f, p, l] = whole[base : base + modes]


def legendre_stage(spectrum, legendre, numbers, place, waves):
    slots, degrees, modes, _ = spectrum.shape
    half = legendre.shape[2]
    lats = 2 * half // waves
    rows = modes * FIELDS * PARTS
    turned = jnp.transpose(spectrum, (0, 3, 2, 1)).reshape(slots, rows, degrees)
    basis = jnp.transpose(legendre, (0, 2, 1))
    chunks = degrees // CHUNK + 1
    tiles = -(-rows // LANES)
    smem = pl.BlockSpec(memory_space=pltpu.SMEM)
    away = pl.BlockSpec(memory_space=pl.ANY)
    return pl.pallas_call(
        legendre_kernel,
        out_shape=[jax.ShapeDtypeStruct((FIELDS, PARTS, lats, modes, slots), jnp.bfloat16)] * waves,
        in_specs=[smem, smem, away, away],
        out_specs=[vmem()] * waves,
        scratch_shapes=[
            pltpu.VMEM((AHEAD + 1, PAIRS, rows, chunks * CHUNK), jnp.bfloat16),
            pltpu.VMEM((AHEAD + 1, 2 * PAIRS, half, degrees), jnp.bfloat16),
            pltpu.VMEM((tiles, 2 * half * slots, LANES), jnp.float32),
            pltpu.SemaphoreType.DMA((AHEAD + 1,)),
        ],
        compiler_params=pltpu.CompilerParams(vmem_limit_bytes=58 << 20),
        cost_estimate=cost(slots * rows * degrees * 2 * half, slots * rows * degrees),
        name="legendre_sums",
    )(numbers, place, turned, basis)


def twiddle_kernel(place_ref, low_cos_ref, low_sin_ref, turn_cos_ref, turn_sin_ref, out_ref):
    slots = low_cos_ref.shape[1]
    shape = (LANES, slots)
    turn_cos = jnp.broadcast_to(turn_cos_ref[0], shape).T
    turn_sin = jnp.broadcast_to(turn_sin_ref[0], shape).T
    cos, sin = low_cos_ref[0], low_sin_ref[0]
    for block in range(out_ref.shape[3] // LANES):
        lanes = pl.ds(block * LANES, LANES)
        out_ref[0, 0, :, lanes] = cos.astype(jnp.bfloat16)
        out_ref[0, 1, :, lanes] = (-sin).astype(jnp.bfloat16)
        cos, sin = cos * turn_cos - sin * turn_sin, sin * turn_cos + cos * turn_sin


def twiddle_stage(numbers, place):
    waves, slots = numbers.shape
    count = NLON // 2

    def angles(residue):
        return (residue % NLON).astype(jnp.float32) * (2.0 * math.pi / NLON)

    low = angles(numbers[:, :, None] * jnp.arange(LANES, dtype=jnp.int32)[None, None, :])
    turn = angles(numbers * LANES)[:, None, :]
    weight = jnp.where(numbers == 0, 1.0, 2.0).astype(jnp.float32)[:, :, None]

    def spec(rows, last):
        return pl.BlockSpec((1, rows, last), lambda i, place_ref: (place_ref[0] ^ i, 0, 0))

    return pl.pallas_call(
        twiddle_kernel,
        out_shape=jax.ShapeDtypeStruct((waves, PARTS, slots, count), jnp.bfloat16),
        grid_spec=pltpu.PrefetchScalarGridSpec(
            num_scalar_prefetch=1,
            grid=(waves,),
            in_specs=[spec(slots, LANES), spec(slots, LANES), spec(1, slots), spec(1, slots)],
            out_specs=pl.BlockSpec((1, PARTS, slots, count), lambda i, _: (i, 0, 0, 0)),
        ),
        compiler_params=pltpu.CompilerParams(vmem_limit_bytes=8 << 20),
        cost_estimate=cost(8 * waves * slots * count, 4 * waves * slots * count),
        name="twiddles",
    )(place, weight * jnp.cos(low), weight * jnp.sin(low), jnp.cos(turn), jnp.sin(turn))


def synthesis_kernel(waves, levs, fields, wave_ref, lev_ref, *refs):
    blocks, (sign_ref, twiddle_ref) = refs[:waves], refs[waves : waves + 2]
    outs, (left, grid) = refs[waves + 2 : -2], refs[-2:]
    _, _, lats, modes, slots = blocks[0].shape
    each = lats * modes
    rows = each * len(fields)
    for d in range(waves):
        sign = sign_ref[wave_ref[0] ^ d]
        for p in range(PARTS):
            lanes = pl.ds((d * PARTS + p) * slots, slots)
            for place, field in enumerate(fields):
                values = blocks[d][field, p].reshape(each, slots)
                left[place * each : (place + 1) * each, lanes] = values
                left[rows + place * each : rows + (place + 1) * each, lanes] = values * sign

    width = NLON // levs
    ratio = width // TILE
    steps = twiddle_ref.shape[3] // TILE
    for step in range(steps):
        right = twiddle_ref[:, :, :, pl.ds(step * TILE, TILE)]
        right = right.reshape(waves * PARTS * slots, TILE)
        result = jnp.dot(left[...], right, preferred_element_type=jnp.float32)
        result = result.astype(jnp.bfloat16)
        for which in range(2):
            owner, inner = divmod(step + which * steps, ratio)
            part = result[which * rows : (which + 1) * rows]
            grid[owner, :rows, pl.ds(inner * TILE, TILE)] = part
    lane = lax.broadcasted_iota(jnp.int32, (modes, LANES), 1)
    for owner in range(levs):
        halos = jnp.zeros((modes, LANES), jnp.float32)
        for k in range(rows // modes):
            own = pl.ds(k * modes, modes)
            east = grid[(owner + 1) % levs, own, :LANES]
            west = grid[(owner - 1) % levs, own, pl.ds(width - LANES, LANES)]
            halo = jnp.where(lane < LANES // 2, east.astype(jnp.float32), west.astype(jnp.float32))
            turned = pltpu.roll(halo, HALO * k, 1) if k else halo
            inside = lax.rem(lane + (LANES + HALO // 2 - HALO * k), LANES) < HALO
            halos = jnp.where(inside, turned, halos)
        for g in range(width // LANES):
            part = halos[8 * g : 8 * g + 8] if 8 * g < modes else jnp.zeros((8, LANES), jnp.float32)
            grid[owner, pl.ds(rows, 8), pl.ds(g * LANES, LANES)] = part.astype(jnp.bfloat16)
    place = lev_ref[0]
    for e in range(levs):
        outs[e][...] = grid[place ^ e]


def synthesis_stage(blocks, sign, twiddle, wave_place, lev_place, levs, fields):
    waves, _, slots, count = twiddle.shape
    _, _, lats, modes, _ = blocks[0].shape
    rows = lats * modes * len(fields)
    width = NLON // levs
    depth = waves * PARTS * slots
    return pl.pallas_call(
        functools.partial(synthesis_kernel, waves, levs, fields),
        out_shape=[jax.ShapeDtypeStruct((rows + 8, width), jnp.bfloat16)] * levs,
        in_specs=[pl.BlockSpec(memory_space=pltpu.SMEM)] * 2 + [vmem()] * (waves + 2),
        out_specs=[vmem()] * levs,
        scratch_shapes=[
            pltpu.VMEM((2 * rows, depth), jnp.bfloat16),
            pltpu.VMEM((levs, rows + 8, width), jnp.bfloat16),
        ],
        compiler_params=pltpu.CompilerParams(vmem_limit_bytes=12 << 20),
        cost_estimate=cost(4 * rows * depth * count, 2 * depth * count),
        name="synthesis",
    )(wave_place, lev_place, *blocks, sign, twiddle)


def three_terms(matrix):
    high = matrix.astype(jnp.bfloat16)
    rest = matrix - high.astype(jnp.float32)
    middle = rest.astype(jnp.bfloat16)
    low = (rest - middle.astype(jnp.float32)).astype(jnp.bfloat16)
    return jnp.concatenate([high, middle, low], axis=0)


def levels_of(terms, place, blocks, gathered, base, modes):
    count = terms.shape[0] // 3
    for e, block in enumerate(blocks):
        start = pl.multiple_of((place ^ e) * modes, modes)
        rows, width = block.shape
        gathered[pl.ds(start, modes), :width] = block[base : base + modes].astype(jnp.float32)
        halos = jnp.concatenate(
            [
                block[rows - 8 :, g * LANES : (g + 1) * LANES].astype(jnp.float32)
                for g in range(modes // 8)
            ],
            axis=0,
        )
        turn = HALO * (base // modes)
        halo = pltpu.roll(halos, LANES - turn, 1) if turn else halos
        gathered[pl.ds(start, modes), pl.ds(width, LANES)] = halo
    rows = gathered[...].astype(jnp.bfloat16)
    result = jnp.dot(terms, rows, preferred_element_type=jnp.float32)
    return result[:count] + (result[count : 2 * count] + result[2 * count :])


def keep_edges(lat, lats, values, odd, pair_ref, diagonal_ref):
    edge = values.astype(jnp.bfloat16)
    if 0 < lat < lats - 1:
        return
    takes_pair = 1 if lat == 0 else 0

    @pl.when(odd == takes_pair)
    def _():
        pair_ref[...] = edge

    @pl.when(odd != takes_pair)
    def _():
        diagonal_ref[...] = edge


def tracer_kernel(modes, odd_ref, lev_ref, vertical_ref, *refs):
    blocks, (field_ref, pair_ref, diagonal_ref, gathered) = refs[:-4], refs[-4:]
    terms = three_terms(vertical_ref[...])
    lats = field_ref.shape[0]
    for lat in range(lats):
        values = levels_of(terms, lev_ref[0], blocks, gathered, lat * modes, modes)
        field_ref[lat] = values
        keep_edges(lat, lats, values, odd_ref[0], pair_ref, diagonal_ref)


def upwind(center, western, eastern, northern, southern, courant_x, courant_y):
    return (
        center
        - jnp.maximum(courant_x, 0.0) * (center - western)
        - jnp.minimum(courant_x, 0.0) * (eastern - center)
        - jnp.maximum(courant_y, 0.0) * (center - northern)
        - jnp.minimum(courant_y, 0.0) * (southern - center)
    )


def row_step(center, northern, southern, courant_x, courant_y):
    width = center.shape[1]
    western, eastern = pltpu.roll(center, 1, 1), pltpu.roll(center, width - 1, 1)
    return upwind(center, western, eastern, northern, southern, courant_x, courant_y)


def outside(takes_pair, odd_ref, end_ref, pair_ref, diagonal_ref):
    pair = pair_ref[...].astype(jnp.float32)
    diagonal = jnp.where(end_ref[0] == 1, 0.0, diagonal_ref[...].astype(jnp.float32))
    return jnp.where(odd_ref[0] == takes_pair, pair, diagonal)


def courants(lev_ref, vertical_ref, blocks, gathered, lats, modes):
    terms = three_terms(vertical_ref[...])

    def of(field, lat):
        base = (field * lats + lat) * modes
        velocity = levels_of(terms, lev_ref[0], blocks, gathered.at[field], base, modes)
        return courant_max * jnp.tanh(velocity)

    return of


def edge_step_kernel(
    modes, odd_ref, end_ref, lev_ref, vertical_ref, tracer_ref, pair_ref, diagonal_ref, *refs
):
    blocks, (x_ref, y_ref, out_ref, next_pair_ref, next_diagonal_ref, gathered) = refs[:-6], refs[-6:]
    lats = tracer_ref.shape[0]
    courant = courants(lev_ref, vertical_ref, blocks, gathered, lats, modes)
    for place, lat in enumerate((0, lats - 1)):
        other = outside(1 - place, odd_ref, end_ref, pair_ref, diagonal_ref)
        northern = other if place == 0 else tracer_ref[lat - 1]
        southern = tracer_ref[lat + 1] if place == 0 else other
        x_ref[place], y_ref[place] = courant(0, lat), courant(1, lat)
        values = row_step(tracer_ref[lat], northern, southern, x_ref[place], y_ref[place])
        out_ref[place] = values
        keep_edges(lat, lats, values, odd_ref[0], next_pair_ref, next_diagonal_ref)


def inner_steps_kernel(modes, lev_ref, vertical_ref, tracer_ref, edge_ref, *refs):
    blocks, (inner_ref, out_ref, x_ref, y_ref, gathered) = refs[:-5], refs[-5:]
    lats = tracer_ref.shape[0]
    width = out_ref.shape[2]
    courant = courants(lev_ref, vertical_ref, blocks, gathered, lats, modes)
    inner = lats - 2
    for place in range(inner):
        lat = place + 1
        x_ref[place], y_ref[place] = courant(0, lat), courant(1, lat)
        inner_ref[place] = row_step(
            tracer_ref[lat], tracer_ref[lat - 1], tracer_ref[lat + 1], x_ref[place], y_ref[place]
        )
    for place in range(inner):
        northern = inner_ref[place - 1] if place > 0 else edge_ref[0]
        southern = inner_ref[place + 1] if place < inner - 1 else edge_ref[1]
        values = row_step(inner_ref[place], northern, southern, x_ref[place], y_ref[place])
        out_ref[place] = values[:, :width]


def last_step_kernel(
    odd_ref, end_ref, edge_ref, inner_ref, done_ref, pair_ref, diagonal_ref, x_ref, y_ref, out_ref
):
    inner, _, width = done_ref.shape
    for place in range(inner):
        out_ref[:, place + 1, :] = done_ref[place]
    for place in range(2):
        other = outside(1 - place, odd_ref, end_ref, pair_ref, diagonal_ref)
        northern = other if place == 0 else inner_ref[inner - 1]
        southern = inner_ref[0] if place == 0 else other
        values = row_step(edge_ref[place], northern, southern, x_ref[place], y_ref[place])
        out_ref[:, place * (inner + 1), :] = values[:, :width]


def local_call(kernel, outs, scratch, *operands):
    smem = pl.BlockSpec(memory_space=pltpu.SMEM)
    return pl.pallas_call(
        kernel,
        out_shape=outs,
        in_specs=[smem if operand.dtype == jnp.int32 else vmem() for operand in operands],
        out_specs=jax.tree.map(lambda _: vmem(), outs),
        scratch_shapes=scratch,
        compiler_params=pltpu.CompilerParams(vmem_limit_bytes=16 << 20),
        cost_estimate=cost(4_000_000, 4_000_000),
    )(*operands)


def exchange(blocks, axis):
    count = lax.axis_size(axis)
    moved = [blocks[0]]
    for d in range(1, count):
        moved.append(lax.ppermute(blocks[d], axis, [(i, i ^ d) for i in range(count)]))
    return moved


def edges(pair, diagonal):
    count = lax.axis_size("wave")
    steps = [(i, i + 1) for i in range(1, count - 1, 2)] + [(0, 0)]
    steps = steps + [(b, a) for a, b in steps[:-1]] + [(count - 1, count - 1)]
    diagonal = lax.ppermute(diagonal, "wave", steps)
    pair = lax.ppermute(pair, "wave", [(i, i ^ 1) for i in range(count)])
    return pair, diagonal


def tiled_body(spectrum, legendre, wave_numbers, vertical):
    waves, levs = lax.axis_size("wave"), lax.axis_size("lev")
    slots, _, modes, _ = spectrum.shape
    levels = vertical.shape[0]
    lats = 2 * legendre.shape[2] // waves
    width = NLON // levs
    wave_place, lev_place = lax.axis_index("wave"), lax.axis_index("lev")
    at_end = (wave_place == 0) | (wave_place == waves - 1)
    odd, at_end = lax.rem(wave_place, 2)[None], at_end.astype(jnp.int32)[None]
    wave_place, lev_place = wave_place[None], lev_place[None]

    fourier = legendre_stage(spectrum, legendre, wave_numbers, wave_place, waves)
    by_wave = wave_numbers.reshape(waves, slots)
    sign = jnp.where(by_wave % 2 == 0, 1.0, -1.0).astype(jnp.bfloat16)[:, None, :]
    twiddle = twiddle_stage(by_wave, wave_place)
    received = exchange(fourier, "wave")
    columns = [
        exchange(
            synthesis_stage(received, sign, twiddle, wave_place, lev_place, levs, fields), "lev"
        )
        for fields in ((2,), (0, 1))
    ]

    whole = jax.ShapeDtypeStruct((lats, levels, width + LANES), jnp.float32)
    row = jax.ShapeDtypeStruct((levels, width + LANES), jnp.bfloat16)
    pair_of_rows = jax.ShapeDtypeStruct((2, *whole.shape[1:]), jnp.float32)
    gathered = (levs * modes, width + LANES)
    tracer, pair, diagonal = local_call(
        functools.partial(tracer_kernel, modes),
        (whole, row, row),
        [pltpu.VMEM(gathered, jnp.float32)],
        odd,
        lev_place,
        vertical,
        *columns[0],
    )
    pair, diagonal = edges(pair, diagonal)
    courant_x, courant_y, edge, pair, diagonal = local_call(
        functools.partial(edge_step_kernel, modes),
        (pair_of_rows, pair_of_rows, pair_of_rows, row, row),
        [pltpu.VMEM((2, *gathered), jnp.float32)],
        odd,
        at_end,
        lev_place,
        vertical,
        tracer,
        pair,
        diagonal,
        *columns[1],
    )
    pair, diagonal = edges(pair, diagonal)
    inner, done = local_call(
        functools.partial(inner_steps_kernel, modes),
        (
            jax.ShapeDtypeStruct((lats - 2, levels, width + LANES), jnp.float32),
            jax.ShapeDtypeStruct((lats - 2, levels, width), jnp.float32),
        ),
        [
            pltpu.VMEM((lats - 2, levels, width + LANES), jnp.float32),
            pltpu.VMEM((lats - 2, levels, width + LANES), jnp.float32),
            pltpu.VMEM((2, *gathered), jnp.float32),
        ],
        lev_place,
        vertical,
        tracer,
        edge,
        *columns[1],
    )
    return local_call(
        last_step_kernel,
        jax.ShapeDtypeStruct((levels, lats, width), jnp.float32),
        [],
        odd,
        at_end,
        edge,
        inner,
        done,
        pair,
        diagonal,
        courant_x,
        courant_y,
    )


def body(spectrum, legendre, wave_numbers, vertical):
    waves, levs = lax.axis_size("wave"), lax.axis_size("lev")
    slots, degrees, modes, _ = spectrum.shape
    tiled = (
        slots % LANES == 0
        and slots % (2 * PAIRS) == 0
        and slots > 2 * PAIRS * AHEAD
        and legendre.shape[2] % 16 == 0
        and modes % 8 == 0
        and degrees % CHUNK == 0
        and waves & (waves - 1) == 0
        and levs & (levs - 1) == 0
        and NLON // levs % TILE == 0
        and levs % 2 == 0
        and modes // 8 * LANES <= NLON // levs
        and 2 * HALO * (2 * legendre.shape[2] // waves) <= LANES
        and 2 * legendre.shape[2] // waves >= 3
    )
    form = tiled_body if tiled else plain_body
    return form(spectrum, legendre, wave_numbers, vertical)


def solution(mesh):
    in_specs = (P("wave", None, "lev", None), P("wave", None, None), P(), P())
    out_specs = P(None, "wave", "lev")
    return jax.shard_map(body, mesh=mesh, in_specs=in_specs, out_specs=out_specs, check_vma=False)
```

```python
import functools
import math

import jax
import jax.numpy as jnp
from jax import lax
from jax.experimental import pallas as pl
from jax.experimental.pallas import tpu as pltpu
from jax.sharding import PartitionSpec as P

NLON = 2048
FIELDS = 3
PARTS = 2
LANES = 128
CHUNK = 256
TILE = 256
PAIRS = 8
HALO = 4
AHEAD = 7

courant_max = 0.45


def padded(block, sides, width, periodic):
    for axis, dim in sides:
        count = lax.axis_size(axis)
        forward = [(i, i + 1) for i in range(count - 1)]
        if periodic:
            forward.append((count - 1, 0))
        backward = [(target, source) for source, target in forward]
        low = lax.ppermute(
            lax.slice_in_dim(block, block.shape[dim] - width, None, axis=dim), axis, forward
        )
        high = lax.ppermute(lax.slice_in_dim(block, 0, width, axis=dim), axis, backward)
        block = jnp.concatenate([low, block, high], axis=dim)
    return block


def twiddles(numbers):
    longitude = jnp.arange(NLON, dtype=jnp.int32)
    residue = numbers[:, None] * longitude[None, :] % NLON
    angles = residue.astype(jnp.float32) * (2.0 * math.pi / NLON)
    weight = jnp.where(numbers == 0, 1.0, 2.0).astype(jnp.float32)[:, None]
    return jnp.stack([weight * jnp.cos(angles), -weight * jnp.sin(angles)]).astype(jnp.bfloat16)


def parity_columns(coefficient, degree, lengths):
    counted = degree < lengths[:, None]
    even_mask = counted & (degree % 2 == 0)
    odd_mask = counted & (degree % 2 == 1)
    return jnp.concatenate(
        [
            jnp.where(even_mask[:, :, None], coefficient, 0),
            jnp.where(odd_mask[:, :, None], coefficient, 0),
        ],
        axis=2,
    )


def padded_sums(coefficient, basis, own_numbers):
    degree_count = coefficient.shape[1]
    degree = jnp.arange(degree_count, dtype=jnp.int32)[None, :]
    masked = parity_columns(coefficient, degree, degree_count - own_numbers)
    return jnp.einsum("skc,ski->sci", masked, basis, preferred_element_type=jnp.float32)


def upwind_core(extended, courant_x, courant_y):
    center = extended[:, 1:-1, 1:-1]
    western = extended[:, 1:-1, :-2]
    eastern = extended[:, 1:-1, 2:]
    northern = extended[:, :-2, 1:-1]
    southern = extended[:, 2:, 1:-1]
    return (
        center
        - jnp.maximum(courant_x, 0.0) * (center - western)
        - jnp.minimum(courant_x, 0.0) * (eastern - center)
        - jnp.maximum(courant_y, 0.0) * (center - northern)
        - jnp.minimum(courant_y, 0.0) * (southern - center)
    )


def plain_body(spectrum, legendre, wave_numbers, vertical):
    slot_count, degree_count, level_count, part_count = spectrum.shape
    columns = level_count * part_count
    coefficient = spectrum.reshape(slot_count, degree_count, columns)
    first_slot = lax.axis_index("wave") * slot_count
    own_numbers = lax.dynamic_slice_in_dim(wave_numbers, first_slot, slot_count)
    partial_sums = padded_sums(coefficient, legendre, own_numbers)
    even_sums = partial_sums[:, :columns]
    odd_sums = partial_sums[:, columns:]
    northern = even_sums + odd_sums
    southern = jnp.flip(even_sums - odd_sums, axis=2)
    fourier = jnp.concatenate([northern, southern], axis=2).astype(jnp.bfloat16)
    received = lax.all_to_all(fourier, "wave", split_axis=2, concat_axis=0, tiled=True)
    lat_count = received.shape[2]
    received = received.reshape(received.shape[0], level_count, FIELDS, PARTS, lat_count)
    twiddle = twiddles(wave_numbers)
    grid_values = jnp.einsum(
        "smfrl,rsj->lmfj", received, twiddle, preferred_element_type=jnp.float32
    ).astype(jnp.bfloat16)
    column_values = lax.all_to_all(grid_values, "lev", split_axis=3, concat_axis=1, tiled=True)
    fields = jnp.einsum(
        "vm,lmfj->fvlj",
        vertical,
        column_values.astype(jnp.float32),
        precision=lax.Precision.HIGHEST,
    )
    courant_x = courant_max * jnp.tanh(fields[0])
    courant_y = courant_max * jnp.tanh(fields[1])
    tracer = fields[2]
    for _ in range(2):
        extended = padded(tracer, (("wave", 1),), 1, False)
        extended = padded(extended, (("lev", 2),), 1, True)
        tracer = upwind_core(extended, courant_x, courant_y)
    return tracer


def vmem():
    return pl.BlockSpec(memory_space=pltpu.VMEM)


def cost(flops, count_bytes):
    return pl.CostEstimate(flops=flops, bytes_accessed=count_bytes, transcendentals=0)


def legendre_kernel(numbers_ref, place_ref, spectrum_ref, legendre_ref, *refs):
    outs, (held, basis_held, sums, arrived) = refs[:-4], refs[-4:]
    waves = len(outs)
    _, _, lats, modes, _ = outs[0].shape
    buffers, pairs, rows, _ = held.shape
    slots, half, degrees = legendre_ref.shape
    chunks = degrees // CHUNK + 1
    steps = slots // (2 * pairs)
    ahead = buffers - 1
    place = place_ref[0]

    def plan(index):
        first = degrees - numbers_ref[place * slots + 2 * index]
        second = degrees - numbers_ref[place * slots + 2 * index + 1]
        return first, second, lax.shift_right_logical(first + (CHUNK - 1), CHUNK.bit_length() - 1)

    def fetch(group, slot):
        pltpu.make_async_copy(
            legendre_ref.at[pl.ds(group * 2 * pairs, 2 * pairs)],
            basis_held.at[slot],
            arrived.at[slot],
        ).start()
        for pair in range(pairs):
            index = group * pairs + pair
            _, _, edge = plan(index)

            def counted(first, index=index, pair=pair):
                for source, start, count in (
                    (2 * index, 0, first),
                    (2 * index + 1, first, chunks - first),
                ):
                    pltpu.make_async_copy(
                        spectrum_ref.at[source, :, pl.ds(0, count * CHUNK)],
                        held.at[slot, pair, :, pl.ds(start * CHUNK, count * CHUNK)],
                        arrived.at[slot],
                    ).start()

            lax.switch(edge - 1, [functools.partial(counted, n) for n in range(1, chunks)])

    for group in range(min(ahead, steps)):
        fetch(group, group)

    def work(step, fetches):
        now = lax.rem(step, buffers)
        for buffer in (held, basis_held):
            pltpu.make_async_copy(buffer.at[now], buffer.at[now], arrived.at[now]).wait()
        if fetches:
            fetch(step + ahead, lax.rem(step + ahead, buffers))
        lane = lax.broadcasted_iota(jnp.int32, (half, CHUNK), 1)
        sign = jnp.where(lane % 2 == 0, 1.0, -1.0).astype(jnp.bfloat16)
        for pair in range(pairs):
            index = step * pairs + pair
            first, second, edge = plan(index)
            columns = []
            for t in range(chunks):
                inside = t < edge
                local = jnp.where(inside, 2 * pair, 2 * pair + 1)
                block = jnp.where(inside, t, t - edge)
                start = pl.multiple_of(block * CHUNK, CHUNK)
                length = jnp.where(inside, first, second) - start
                values = basis_held[now, local, :, pl.ds(start, CHUNK)]
                own = jnp.where(inside, length, 0)
                own_mask = jnp.where(lane < own, 1.0, 0.0).astype(jnp.bfloat16)
                other_mask = jnp.where(lane < length - own, 1.0, 0.0).astype(jnp.bfloat16)
                flip = values * sign
                columns.append(
                    jnp.concatenate([values * own_mask, flip * own_mask, values * other_mask, flip * other_mask], axis=0)
                )
            result = lax.dot_general(
                jnp.concatenate(columns, axis=1),
                held[now, pair],
                (((1,), (1,)), ((), ())),
                preferred_element_type=jnp.float32,
            )
            for which in range(2):
                part = result[which * 2 * half : (which + 1) * 2 * half]
                for low in range(0, rows, LANES):
                    width = min(LANES, rows - low)
                    sums[low // LANES, pl.ds(2 * index + which, 2 * half, stride=slots), :width] = (
                        part[:, low : low + width]
                    )

    lax.fori_loop(0, steps - ahead, lambda step, _: work(step, True), None)
    lax.fori_loop(steps - ahead, steps, lambda step, _: work(step, False), None)

    for d in range(waves):
        for l in range(lats):
            lat = (place ^ d) * lats + l
            row = jnp.where(lat < half, lat, 3 * half - 1 - lat)
            turned = [
                sums[low // LANES, pl.ds(pl.multiple_of(row * slots, slots), slots), :].T.astype(jnp.bfloat16) for low in range(0, rows, LANES)
            ]
            whole = jnp.concatenate(turned, axis=0)
            for f in range(FIELDS):
                for p in range(PARTS):
                    base = (f * PARTS + p) * modes
                    outs[d][f, p, l] = whole[base : base + modes]


def legendre_stage(spectrum, legendre, numbers, place, waves):
    slots, degrees, modes, _ = spectrum.shape
    half = legendre.shape[2]
    lats = 2 * half // waves
    rows = modes * FIELDS * PARTS
    turned = jnp.transpose(spectrum, (0, 3, 2, 1)).reshape(slots, rows, degrees)
    basis = jnp.transpose(legendre, (0, 2, 1))
    chunks = degrees // CHUNK + 1
    tiles = -(-rows // LANES)
    smem = pl.BlockSpec(memory_space=pltpu.SMEM)
    away = pl.BlockSpec(memory_space=pl.ANY)
    return pl.pallas_call(
        legendre_kernel,
        out_shape=[jax.ShapeDtypeStruct((FIELDS, PARTS, lats, modes, slots), jnp.bfloat16)] * waves,
        in_specs=[smem, smem, away, away],
        out_specs=[vmem()] * waves,
        scratch_shapes=[
            pltpu.VMEM((AHEAD + 1, PAIRS, rows, chunks * CHUNK), jnp.bfloat16),
            pltpu.VMEM((AHEAD + 1, 2 * PAIRS, half, degrees), jnp.bfloat16),
            pltpu.VMEM((tiles, 2 * half * slots, LANES), jnp.float32),
            pltpu.SemaphoreType.DMA((AHEAD + 1,)),
        ],
        compiler_params=pltpu.CompilerParams(vmem_limit_bytes=58 << 20),
        cost_estimate=cost(slots * rows * degrees * 2 * half, slots * rows * degrees),
        name="legendre_sums",
    )(numbers, place, turned, basis)


def twiddle_kernel(place_ref, low_cos_ref, low_sin_ref, turn_cos_ref, turn_sin_ref, out_ref):
    slots = low_cos_ref.shape[1]
    shape = (LANES, slots)
    turn_cos = jnp.broadcast_to(turn_cos_ref[0], shape).T
    turn_sin = jnp.broadcast_to(turn_sin_ref[0], shape).T
    cos, sin = low_cos_ref[0], low_sin_ref[0]
    for block in range(out_ref.shape[3] // LANES):
        lanes = pl.ds(block * LANES, LANES)
        out_ref[0, 0, :, lanes] = cos.astype(jnp.bfloat16)
        out_ref[0, 1, :, lanes] = (-sin).astype(jnp.bfloat16)
        cos, sin = cos * turn_cos - sin * turn_sin, sin * turn_cos + cos * turn_sin


def twiddle_stage(numbers, place):
    waves, slots = numbers.shape
    count = NLON // 2

    def angles(residue):
        return (residue % NLON).astype(jnp.float32) * (2.0 * math.pi / NLON)

    low = angles(numbers[:, :, None] * jnp.arange(LANES, dtype=jnp.int32)[None, None, :])
    turn = angles(numbers * LANES)[:, None, :]
    weight = jnp.where(numbers == 0, 1.0, 2.0).astype(jnp.float32)[:, :, None]

    def spec(rows, last):
        return pl.BlockSpec((1, rows, last), lambda i, place_ref: (place_ref[0] ^ i, 0, 0))

    return pl.pallas_call(
        twiddle_kernel,
        out_shape=jax.ShapeDtypeStruct((waves, PARTS, slots, count), jnp.bfloat16),
        grid_spec=pltpu.PrefetchScalarGridSpec(
            num_scalar_prefetch=1,
            grid=(waves,),
            in_specs=[spec(slots, LANES), spec(slots, LANES), spec(1, slots), spec(1, slots)],
            out_specs=pl.BlockSpec((1, PARTS, slots, count), lambda i, _: (i, 0, 0, 0)),
        ),
        compiler_params=pltpu.CompilerParams(vmem_limit_bytes=8 << 20),
        cost_estimate=cost(8 * waves * slots * count, 4 * waves * slots * count),
        name="twiddles",
    )(place, weight * jnp.cos(low), weight * jnp.sin(low), jnp.cos(turn), jnp.sin(turn))


def synthesis_kernel(waves, levs, fields, wave_ref, lev_ref, *refs):
    blocks, (sign_ref, twiddle_ref) = refs[:waves], refs[waves : waves + 2]
    outs, (left, grid) = refs[waves + 2 : -2], refs[-2:]
    _, _, lats, modes, slots = blocks[0].shape
    each = lats * modes
    rows = each * len(fields)
    for d in range(waves):
        sign = sign_ref[wave_ref[0] ^ d]
        for p in range(PARTS):
            lanes = pl.ds((d * PARTS + p) * slots, slots)
            for place, field in enumerate(fields):
                values = blocks[d][field, p].reshape(each, slots)
                left[place * each : (place + 1) * each, lanes] = values
                left[rows + place * each : rows + (place + 1) * each, lanes] = values * sign

    width = NLON // levs
    ratio = width // TILE
    steps = twiddle_ref.shape[3] // TILE
    for step in range(steps):
        right = twiddle_ref[:, :, :, pl.ds(step * TILE, TILE)]
        right = right.reshape(waves * PARTS * slots, TILE)
        result = jnp.dot(left[...], right, preferred_element_type=jnp.float32)
        result = result.astype(jnp.bfloat16)
        for which in range(2):
            owner, inner = divmod(step + which * steps, ratio)
            part = result[which * rows : (which + 1) * rows]
            grid[owner, :rows, pl.ds(inner * TILE, TILE)] = part
    lane = lax.broadcasted_iota(jnp.int32, (modes, LANES), 1)
    for owner in range(levs):
        halos = jnp.zeros((modes, LANES), jnp.float32)
        for k in range(rows // modes):
            own = pl.ds(k * modes, modes)
            east = grid[(owner + 1) % levs, own, :LANES]
            west = grid[(owner - 1) % levs, own, pl.ds(width - LANES, LANES)]
            halo = jnp.where(lane < LANES // 2, east.astype(jnp.float32), west.astype(jnp.float32))
            turned = pltpu.roll(halo, HALO * k, 1) if k else halo
            inside = lax.rem(lane + (LANES + HALO // 2 - HALO * k), LANES) < HALO
            halos = jnp.where(inside, turned, halos)
        for g in range(width // LANES):
            part = halos[8 * g : 8 * g + 8] if 8 * g < modes else jnp.zeros((8, LANES), jnp.float32)
            grid[owner, pl.ds(rows, 8), pl.ds(g * LANES, LANES)] = part.astype(jnp.bfloat16)
    place = lev_ref[0]
    for e in range(levs):
        outs[e][...] = grid[place ^ e]


def synthesis_stage(blocks, sign, twiddle, wave_place, lev_place, levs, fields):
    waves, _, slots, count = twiddle.shape
    _, _, lats, modes, _ = blocks[0].shape
    rows = lats * modes * len(fields)
    width = NLON // levs
    depth = waves * PARTS * slots
    return pl.pallas_call(
        functools.partial(synthesis_kernel, waves, levs, fields),
        out_shape=[jax.ShapeDtypeStruct((rows + 8, width), jnp.bfloat16)] * levs,
        in_specs=[pl.BlockSpec(memory_space=pltpu.SMEM)] * 2 + [vmem()] * (waves + 2),
        out_specs=[vmem()] * levs,
        scratch_shapes=[
            pltpu.VMEM((2 * rows, depth), jnp.bfloat16),
            pltpu.VMEM((levs, rows + 8, width), jnp.bfloat16),
        ],
        compiler_params=pltpu.CompilerParams(vmem_limit_bytes=12 << 20),
        cost_estimate=cost(4 * rows * depth * count, 2 * depth * count),
        name="synthesis",
    )(wave_place, lev_place, *blocks, sign, twiddle)


def three_terms(matrix):
    high = matrix.astype(jnp.bfloat16)
    rest = matrix - high.astype(jnp.float32)
    middle = rest.astype(jnp.bfloat16)
    low = (rest - middle.astype(jnp.float32)).astype(jnp.bfloat16)
    return jnp.concatenate([high, middle, low], axis=0)


def levels_of(terms, place, blocks, gathered, base, modes):
    count = terms.shape[0] // 3
    for e, block in enumerate(blocks):
        start = pl.multiple_of((place ^ e) * modes, modes)
        rows, width = block.shape
        gathered[pl.ds(start, modes), :width] = block[base : base + modes].astype(jnp.float32)
        halos = jnp.concatenate(
            [
                block[rows - 8 :, g * LANES : (g + 1) * LANES].astype(jnp.float32)
                for g in range(modes // 8)
            ],
            axis=0,
        )
        turn = HALO * (base // modes)
        halo = pltpu.roll(halos, LANES - turn, 1) if turn else halos
        gathered[pl.ds(start, modes), pl.ds(width, LANES)] = halo
    rows = gathered[...].astype(jnp.bfloat16)
    result = jnp.dot(terms, rows, preferred_element_type=jnp.float32)
    return result[:count] + (result[count : 2 * count] + result[2 * count :])


def keep_edges(lat, lats, values, odd, pair_ref, diagonal_ref):
    edge = values[:, : pair_ref.shape[1]].astype(jnp.bfloat16)
    if 0 < lat < lats - 1:
        return
    takes_pair = 1 if lat == 0 else 0

    @pl.when(odd == takes_pair)
    def _():
        pair_ref[...] = edge

    @pl.when(odd != takes_pair)
    def _():
        diagonal_ref[...] = edge


def tracer_kernel(modes, odd_ref, lev_ref, vertical_ref, *refs):
    blocks, (field_ref, pair_ref, diagonal_ref, gathered) = refs[:-4], refs[-4:]
    terms = three_terms(vertical_ref[...])
    lats = field_ref.shape[0]
    for lat in range(lats):
        values = levels_of(terms, lev_ref[0], blocks, gathered, lat * modes, modes)
        field_ref[lat] = values
        keep_edges(lat, lats, values, odd_ref[0], pair_ref, diagonal_ref)


def upwind(center, western, eastern, northern, southern, courant_x, courant_y):
    return (
        center
        - jnp.maximum(courant_x, 0.0) * (center - western)
        - jnp.minimum(courant_x, 0.0) * (eastern - center)
        - jnp.maximum(courant_y, 0.0) * (center - northern)
        - jnp.minimum(courant_y, 0.0) * (southern - center)
    )


def row_step(center, northern, southern, courant_x, courant_y, kept=None):
    width = center.shape[1]
    western, eastern = pltpu.roll(center, 1, 1), pltpu.roll(center, width - 1, 1)
    rows = (center, western, eastern, northern, southern, courant_x, courant_y)
    return upwind(*(row[:, :kept] for row in rows))


def outside(takes_pair, odd_ref, end_ref, pair_ref, diagonal_ref):
    pair = pair_ref[...].astype(jnp.float32)
    diagonal = jnp.where(end_ref[0] == 1, 0.0, diagonal_ref[...].astype(jnp.float32))
    return jnp.where(odd_ref[0] == takes_pair, pair, diagonal)


def courants(lev_ref, vertical_ref, blocks, gathered, lats, modes):
    terms = three_terms(vertical_ref[...])

    def of(field, lat):
        base = (field * lats + lat) * modes
        velocity = levels_of(terms, lev_ref[0], blocks, gathered.at[field], base, modes)
        return courant_max * jnp.tanh(velocity)

    return of


def edge_step_kernel(
    modes, odd_ref, end_ref, lev_ref, vertical_ref, tracer_ref, pair_ref, diagonal_ref, *refs
):
    blocks, (x_ref, y_ref, out_ref, next_pair_ref, next_diagonal_ref, gathered) = refs[:-6], refs[-6:]
    lats = tracer_ref.shape[0]
    courant = courants(lev_ref, vertical_ref, blocks, gathered, lats, modes)
    for place, lat in enumerate((0, lats - 1)):
        other = outside(1 - place, odd_ref, end_ref, pair_ref, diagonal_ref)
        northern = other if place == 0 else tracer_ref[lat - 1]
        southern = tracer_ref[lat + 1] if place == 0 else other
        x_ref[place], y_ref[place] = courant(0, lat), courant(1, lat)
        values = row_step(tracer_ref[lat], northern, southern, x_ref[place], y_ref[place])
        out_ref[place] = values
        keep_edges(lat, lats, values, odd_ref[0], next_pair_ref, next_diagonal_ref)


def inner_steps_kernel(modes, lev_ref, vertical_ref, tracer_ref, edge_ref, *refs):
    blocks, (inner_ref, out_ref, x_ref, y_ref, gathered) = refs[:-5], refs[-5:]
    lats = tracer_ref.shape[0]
    width = out_ref.shape[2]
    courant = courants(lev_ref, vertical_ref, blocks, gathered, lats, modes)
    inner = lats - 2
    for place in range(inner):
        lat = place + 1
        x_ref[place], y_ref[place] = courant(0, lat), courant(1, lat)
        inner_ref[place] = row_step(
            tracer_ref[lat], tracer_ref[lat - 1], tracer_ref[lat + 1], x_ref[place], y_ref[place]
        )
    for place in range(inner):
        northern = inner_ref[place - 1] if place > 0 else edge_ref[0]
        southern = inner_ref[place + 1] if place < inner - 1 else edge_ref[1]
        out_ref[place] = row_step(
            inner_ref[place], northern, southern, x_ref[place], y_ref[place], width
        )


def last_step_kernel(
    odd_ref, end_ref, edge_ref, inner_ref, done_ref, pair_ref, diagonal_ref, x_ref, y_ref, out_ref
):
    inner, _, width = done_ref.shape
    for place in range(inner):
        out_ref[:, place + 1, :] = done_ref[place]
    for place in range(2):
        other = outside(1 - place, odd_ref, end_ref, pair_ref, diagonal_ref)
        northern = other if place == 0 else inner_ref[inner - 1]
        southern = inner_ref[0] if place == 0 else other
        values = row_step(edge_ref[place], northern, southern, x_ref[place], y_ref[place], width)
        out_ref[:, place * (inner + 1), :] = values


def local_call(kernel, outs, scratch, *operands):
    smem = pl.BlockSpec(memory_space=pltpu.SMEM)
    return pl.pallas_call(
        kernel,
        out_shape=outs,
        in_specs=[smem if operand.dtype == jnp.int32 else vmem() for operand in operands],
        out_specs=jax.tree.map(lambda _: vmem(), outs),
        scratch_shapes=scratch,
        compiler_params=pltpu.CompilerParams(vmem_limit_bytes=16 << 20),
        cost_estimate=cost(4_000_000, 4_000_000),
    )(*operands)


def exchange(blocks, axis):
    count = lax.axis_size(axis)
    moved = [blocks[0]]
    for d in range(1, count):
        moved.append(lax.ppermute(blocks[d], axis, [(i, i ^ d) for i in range(count)]))
    return moved


def edges(pair, diagonal):
    count = lax.axis_size("wave")
    steps = [(i, i + 1) for i in range(1, count - 1, 2)] + [(0, 0)]
    steps = steps + [(b, a) for a, b in steps[:-1]] + [(count - 1, count - 1)]
    diagonal = lax.ppermute(diagonal, "wave", steps)
    pair = lax.ppermute(pair, "wave", [(i, i ^ 1) for i in range(count)])
    return pair, diagonal


def tiled_body(spectrum, legendre, wave_numbers, vertical):
    waves, levs = lax.axis_size("wave"), lax.axis_size("lev")
    slots, _, modes, _ = spectrum.shape
    levels = vertical.shape[0]
    lats = 2 * legendre.shape[2] // waves
    width = NLON // levs
    wave_place, lev_place = lax.axis_index("wave"), lax.axis_index("lev")
    at_end = (wave_place == 0) | (wave_place == waves - 1)
    odd, at_end = lax.rem(wave_place, 2)[None], at_end.astype(jnp.int32)[None]
    wave_place, lev_place = wave_place[None], lev_place[None]

    fourier = legendre_stage(spectrum, legendre, wave_numbers, wave_place, waves)
    by_wave = wave_numbers.reshape(waves, slots)
    sign = jnp.where(by_wave % 2 == 0, 1.0, -1.0).astype(jnp.bfloat16)[:, None, :]
    twiddle = twiddle_stage(by_wave, wave_place)
    received = exchange(fourier, "wave")
    columns = [
        exchange(
            synthesis_stage(received, sign, twiddle, wave_place, lev_place, levs, fields), "lev"
        )
        for fields in ((2,), (0, 1))
    ]

    whole = jax.ShapeDtypeStruct((lats, levels, width + LANES), jnp.float32)
    row = jax.ShapeDtypeStruct((levels, width + LANES), jnp.bfloat16)
    own_row = jax.ShapeDtypeStruct((levels, width), jnp.bfloat16)
    pair_of_rows = jax.ShapeDtypeStruct((2, *whole.shape[1:]), jnp.float32)
    gathered = (levs * modes, width + LANES)
    tracer, pair, diagonal = local_call(
        functools.partial(tracer_kernel, modes),
        (whole, row, row),
        [pltpu.VMEM(gathered, jnp.float32)],
        odd,
        lev_place,
        vertical,
        *columns[0],
    )
    pair, diagonal = edges(pair, diagonal)
    courant_x, courant_y, edge, pair, diagonal = local_call(
        functools.partial(edge_step_kernel, modes),
        (pair_of_rows, pair_of_rows, pair_of_rows, own_row, own_row),
        [pltpu.VMEM((2, *gathered), jnp.float32)],
        odd,
        at_end,
        lev_place,
        vertical,
        tracer,
        pair,
        diagonal,
        *columns[1],
    )
    pair, diagonal = edges(pair, diagonal)
    inner, done = local_call(
        functools.partial(inner_steps_kernel, modes),
        (
            jax.ShapeDtypeStruct((lats - 2, levels, width + LANES), jnp.float32),
            jax.ShapeDtypeStruct((lats - 2, levels, width), jnp.float32),
        ),
        [
            pltpu.VMEM((lats - 2, levels, width + LANES), jnp.float32),
            pltpu.VMEM((lats - 2, levels, width + LANES), jnp.float32),
            pltpu.VMEM((2, *gathered), jnp.float32),
        ],
        lev_place,
        vertical,
        tracer,
        edge,
        *columns[1],
    )
    return local_call(
        last_step_kernel,
        jax.ShapeDtypeStruct((levels, lats, width), jnp.float32),
        [],
        odd,
        at_end,
        edge,
        inner,
        done,
        pair,
        diagonal,
        courant_x,
        courant_y,
    )


def body(spectrum, legendre, wave_numbers, vertical):
    waves, levs = lax.axis_size("wave"), lax.axis_size("lev")
    slots, degrees, modes, _ = spectrum.shape
    tiled = (
        slots % LANES == 0
        and slots % (2 * PAIRS) == 0
        and slots > 2 * PAIRS * AHEAD
        and legendre.shape[2] % 16 == 0
        and modes % 8 == 0
        and degrees % CHUNK == 0
        and waves & (waves - 1) == 0
        and levs & (levs - 1) == 0
        and NLON // levs % TILE == 0
        and levs % 2 == 0
        and modes // 8 * LANES <= NLON // levs
        and 2 * HALO * (2 * legendre.shape[2] // waves) <= LANES
        and 2 * legendre.shape[2] // waves >= 3
    )
    form = tiled_body if tiled else plain_body
    return form(spectrum, legendre, wave_numbers, vertical)


def solution(mesh):
    in_specs = (P("wave", None, "lev", None), P("wave", None, None), P(), P())
    out_specs = P(None, "wave", "lev")
    return jax.shard_map(body, mesh=mesh, in_specs=in_specs, out_specs=out_specs, check_vma=False)
```
